256 devices in a mesh: lon: 16 (over y, x_hi, core), lat: 16 (over z, x_lo).
Axes of the slice: x: 4 (x_hi: 2, x_lo: 2; x = x_hi * 2 + x_lo), y: 4, z: 8, core: 2. Of those that a mesh axis runs over, the one named last changes fastest.
Arguments:
- fine_field: bfloat16 [192, 288, 512], P('lon', 'lat'), may hold values from -6 to 6
- qkv_weight: bfloat16 [512, 1536], replicated, may hold values from -4 to 4
- out_weight: bfloat16 [512, 512], replicated, may hold values from -0.25 to 0.25
- gain_fine: float32 [512], replicated, may hold values from 0.25 to 1.75
- gain_merge: float32 [2048], replicated, may hold values from 0.25 to 1.75
- up_weight: bfloat16 [2048, 8192], P(None, 'lat'), may hold values from -0.125 to 0.125
- down_weight: bfloat16 [8192, 2048], P('lat'), may hold values from -0.0625 to 0.0625
- cotangent: bfloat16 [96, 144, 2048], P('lon', 'lat'), may hold values from -6 to 6
Outputs:
- bottleneck: bfloat16 [96, 144, 2048], P('lon', 'lat')
- grad_field: float32 [192, 288, 512], P('lon', 'lat')
- grad_qkv: float32 [512, 1536], replicated
- grad_out: float32 [512, 512], replicated
- grad_gain_fine: float32 [512], replicated
- grad_gain_merge: float32 [2048], replicated
- grad_up: float32 [2048, 8192], P('lon', 'lat')
- grad_down: float32 [8192, 2048], P('lat', 'lon')
The draws below stay inside these ranges and needn't reach their ends.
All inputs are finite; a program needn't handle non-finite values.
Results may differ from the reference program's by a relative error of at most 0.023.
Values may be sent and summed in bfloat16 or wider, within the bound.
No kernel may reach another device: no remote copies, remote signals or barrier semaphores. Data moves between devices by JAX's collectives and lax.ppermute only.
A program may use at most 128 MiB of HBM per device.

```python
import math
import jax
import jax.numpy as jnp
from jax import lax

C = 512
BC = 2048
FF = 8192
HEADS = 8
WLON = 12
WLAT = 6
NLON = 192
NLAT = 288
N_LAT = 16


def draw_qkv_weight(key, part):
    base = jnp.clip(jax.random.normal(key, (C, 3 * C), jnp.float32), -6.0, 6.0) / math.sqrt(C)
    return jnp.clip(base, -4.0, 4.0).astype(jnp.bfloat16)


def block_scale(key, extent, pieces, low, high):
    def one(axis_at, blocks):
        heights = jax.random.uniform(jax.random.fold_in(jax.random.fold_in(key, 6), axis_at), (blocks,), jnp.float32, low / len(pieces), high / len(pieces))
        return jnp.repeat(jnp.exp(heights), extent[axis_at] // blocks).reshape((-1,) + (1,) * (len(extent) - axis_at - 1))

    gain = one(*pieces[0])
    for cut in pieces[1:]:
        gain = gain * one(*cut)
    return gain


def noise(key, shape, spread, most, shards=(), held_as=jnp.bfloat16):
    loudness = block_scale(key, shape, shards, -0.22, 0.18) if shards else 1.0
    drawn = jax.random.normal(key, shape, jnp.float32) * spread * loudness
    return jnp.minimum(jnp.maximum(drawn, -most), most).astype(held_as)


def setup_inputs(seed: int = 0) -> dict:
    key_list = jax.random.split(jax.random.key(seed), 9)
    return {
        "fine_field": noise(key_list[0], (NLON, NLAT, C), 1.0, 6.0, ((0, 16), (1, 16))),
        "qkv_weight": draw_qkv_weight(jax.random.fold_in(key_list[8], 71), 0),
        "out_weight": noise(key_list[2], (C, C), C ** -0.5, 0.25),
        "gain_fine": jnp.clip(1.0 + 0.15 * jax.random.normal(key_list[3], (C,), jnp.float32), 0.25, 1.75),
        "gain_merge": jnp.clip(1.0 + 0.15 * jax.random.normal(key_list[4], (BC,), jnp.float32), 0.25, 1.75),
        "up_weight": noise(key_list[5], (BC, FF), BC ** -0.5, 0.125, ((1, 16),)),
        "down_weight": noise(key_list[6], (FF, BC), FF ** -0.5, 0.0625, ((0, 16),)),
        "cotangent": noise(key_list[7], (NLON // 2, NLAT // 2, BC), 1.0, 6.0, ((0, 16), (1, 16))),
    }


EPSILON = 1e-05

def layer_norm(values, gain_vec):
    average = lax.optimization_barrier(jnp.mean(values, axis=-1, keepdims=True))
    centred = values - average
    variance = lax.optimization_barrier(jnp.mean(centred * centred, axis=-1, keepdims=True))
    return centred * lax.rsqrt(variance + EPSILON) * gain_vec

def contract_rows(first_arg, second_arg):
    return lax.dot_general(first_arg, second_arg, (((0,), (0,)), ((), ())), preferred_element_type=jnp.float32)

def contract_cols(first_arg, second_arg):
    return lax.dot_general(first_arg, second_arg, (((1,), (1,)), ((), ())), preferred_element_type=jnp.float32)

def to_windows(field):
    lon_size, lat_size, channels = field.shape
    blocked = field.reshape(lon_size // WLON, WLON, lat_size // WLAT, WLAT, channels)
    return blocked.transpose(0, 2, 1, 3, 4).reshape(-1, WLON * WLAT, channels)

def from_windows(windows, lon_size, lat_size):
    channels = windows.shape[-1]
    blocked = windows.reshape(lon_size // WLON, lat_size // WLAT, WLON, WLAT, channels)
    return blocked.transpose(0, 2, 1, 3, 4).reshape(lon_size, lat_size, channels)

def merge_layout(field):
    lon_size, lat_size, channels = field.shape
    blocked = field.reshape(lon_size // 2, 2, lat_size // 2, 2, channels).transpose(0, 2, 1, 3, 4)
    return blocked.reshape(lon_size // 2 * (lat_size // 2), 4 * channels)

def split_layout(merged_rows, lon_size, lat_size):
    channels = merged_rows.shape[1] // 4
    blocked = merged_rows.reshape(lon_size // 2, lat_size // 2, 2, 2, channels).transpose(0, 2, 1, 3, 4)
    return blocked.reshape(lon_size, lat_size, channels)

def attention_core(mixed_qkv):
    window_count, window_size, triple = mixed_qkv.shape
    channels = triple // 3
    head_size = channels // HEADS
    split_parts = mixed_qkv.astype(jnp.float32).reshape(window_count, window_size, 3, HEADS, head_size)
    scores = jnp.einsum('wqhd,wkhd->whqk', split_parts[:, :, 0], split_parts[:, :, 1]) / math.sqrt(head_size)
    weights = jax.nn.softmax(scores, axis=-1).astype(jnp.bfloat16)
    mixed_out = jnp.einsum('whqk,wkhd->wqhd', weights.astype(jnp.float32), split_parts[:, :, 2])
    return mixed_out.astype(jnp.bfloat16).reshape(window_count, window_size, channels)

def attention_forward(windows, qkv_weight, out_weight, gain_vec):
    window_count, window_size, channels = windows.shape
    normed_f, norm_pull = jax.vjp(layer_norm, windows.astype(jnp.float32), gain_vec)
    normed = normed_f.astype(jnp.bfloat16).reshape(window_count * window_size, channels)
    mixed_qkv = jnp.dot(normed, qkv_weight, preferred_element_type=jnp.float32).astype(jnp.bfloat16)
    heads_out, core_pull = jax.vjp(attention_core, mixed_qkv.reshape(window_count, window_size, 3 * channels))
    flat_out = heads_out.reshape(window_count * window_size, channels)
    attended = jnp.dot(flat_out, out_weight, preferred_element_type=jnp.float32)
    return (attended.reshape(window_count, window_size, channels), (norm_pull, core_pull, normed, flat_out))

def attention_backward(saved_state, d_attended, qkv_weight, out_weight):
    norm_pull, core_pull, normed, flat_out = saved_state
    window_count, window_size, channels = d_attended.shape
    d_flat = d_attended.reshape(window_count * window_size, channels).astype(jnp.bfloat16)
    grad_out = contract_rows(flat_out, d_flat)
    d_heads = contract_cols(d_flat, out_weight).astype(jnp.bfloat16)
    d_mixed = core_pull(d_heads.reshape(window_count, window_size, channels))[0]
    d_mixed = d_mixed.reshape(window_count * window_size, 3 * channels)
    grad_qkv = contract_rows(normed, d_mixed)
    d_normed = contract_cols(d_mixed, qkv_weight)
    d_windows, grad_gain = norm_pull(d_normed.reshape(window_count, window_size, channels))
    return (d_windows, grad_qkv, grad_out, grad_gain)

def reference(fine_field, qkv_weight, out_weight, gain_fine, gain_merge, up_weight, down_weight, cotangent):
    margin = WLON // 2
    rolled = jnp.roll(fine_field, margin, axis=0)
    attended, saved_state = attention_forward(to_windows(rolled), qkv_weight, out_weight, gain_fine)
    branch = jnp.roll(from_windows(attended, NLON, NLAT), -margin, axis=0)
    field_out = (fine_field.astype(jnp.float32) + branch).astype(jnp.bfloat16)
    merge_rows = merge_layout(field_out).astype(jnp.float32)
    merged_f, merge_pull = jax.vjp(layer_norm, merge_rows, gain_merge)
    merged = merged_f.astype(jnp.bfloat16)
    grad_rows = cotangent.reshape(merged.shape)
    hidden_share = FF // N_LAT

    def hidden_block(carry, block_index):
        first_unit = block_index * hidden_share
        up_part = lax.dynamic_slice_in_dim(up_weight, first_unit, hidden_share, 1)
        down_part = lax.dynamic_slice_in_dim(down_weight, first_unit, hidden_share, 0)
        pre_act = jnp.dot(merged, up_part, preferred_element_type=jnp.float32)
        activation, gelu_pull = jax.vjp(jax.nn.gelu, pre_act)
        act_low = activation.astype(jnp.bfloat16)
        block_term = jnp.dot(act_low, down_part, preferred_element_type=jnp.float32)
        block_term = block_term.astype(jnp.bfloat16).astype(jnp.float32)
        d_act = contract_cols(grad_rows, down_part)
        d_pre = gelu_pull(d_act)[0].astype(jnp.bfloat16)
        back_term = contract_cols(d_pre, up_part).astype(jnp.bfloat16).astype(jnp.float32)
        grad_up_part = contract_rows(merged, d_pre)
        grad_down_part = contract_rows(act_low, grad_rows)
        return ((carry[0] + block_term, carry[1] + back_term), (grad_up_part, grad_down_part))
    zero_rows = jnp.zeros(merged.shape, jnp.float32)
    (summed, back_sum), (grads_up, grads_down) = lax.scan(hidden_block, (zero_rows, zero_rows), jnp.arange(N_LAT, dtype=jnp.int32))
    bottleneck = (merged.astype(jnp.float32) + summed).astype(jnp.bfloat16).reshape(cotangent.shape)
    grad_up = grads_up.transpose(1, 0, 2).reshape(BC, FF)
    grad_down = grads_down.reshape(FF, BC)
    d_merged = grad_rows.astype(jnp.float32) + back_sum
    d_rows, grad_gain_merge = merge_pull(d_merged)
    d_field = split_layout(d_rows, NLON, NLAT)
    d_rolled = jnp.roll(d_field, margin, axis=0)
    d_windows, grad_qkv, grad_out, grad_gain_fine = attention_backward(saved_state, to_windows(d_rolled), qkv_weight, out_weight)
    grad_field = d_field + jnp.roll(from_windows(d_windows, NLON, NLAT), -margin, axis=0)
    return (bottleneck, grad_field, grad_qkv, grad_out, grad_gain_fine, grad_gain_merge, grad_up, grad_down)
```

```python
import math

import jax
import jax.numpy as jnp
import numpy as np
from jax import lax
from jax.experimental import pallas as pl
from jax.experimental.pallas import tpu as pltpu
from jax.sharding import Mesh
from jax.sharding import PartitionSpec as P

HEADS = 8
WLON = 12
WLAT = 6
MARGIN = WLON // 2
EPSILON = 1e-05
LON = ("y", "xh", "c")
LAT = ("z", "xl")
PLANE = ("y", "xh", "xl")
BF = jnp.bfloat16
F32 = jnp.float32
PAD = 56
BAND = 224
FRAME = 2 * BAND


def shift(block, axis, distance):
    size = lax.axis_size(axis)
    return lax.ppermute(block, axis, [(i, (i + distance) % size) for i in range(size)])


def swap(block, axis, bit=1):
    size = lax.axis_size(axis)
    return lax.ppermute(block, axis, [(i, i ^ bit) for i in range(size)])


def add_low(first_arg, second_arg):
    return (first_arg.astype(F32) + second_arg.astype(F32)).astype(BF)


def gather_around(block, axis):
    size = lax.axis_size(axis)
    width = block.shape[1] // 2
    got = {0: block}
    behind = ahead = block
    for step in range(1, size // 2):
        behind = shift(behind, axis, 1)
        ahead = shift(ahead, axis, -1)
        got[size - step] = behind
        got[step] = ahead
    got[size // 2] = jnp.concatenate(
        [shift(behind[:, :width], axis, 1), shift(ahead[:, width:], axis, -1)], axis=1
    )
    return [got[k] for k in range(size)]


def scatter_around(terms, axis):
    size = lax.axis_size(axis)
    half = size // 2
    width = terms[0].shape[1] // 2
    up = shift(terms[half][:, :width], axis, 1)
    down = shift(terms[half][:, width:], axis, -1)
    up = jnp.concatenate([add_low(terms[half - 1][:, :width], up), terms[half - 1][:, width:]], 1)
    down = jnp.concatenate(
        [terms[half + 1][:, :width], add_low(terms[half + 1][:, width:], down)], 1
    )
    for step in range(half - 2, -1, -1):
        up = shift(up, axis, 1)
        down = shift(down, axis, -1)
        if step:
            up = add_low(terms[step], up)
            down = add_low(terms[size - step], down)
    return up, down


def contract_rows(first_arg, second_arg):
    return lax.dot_general(
        first_arg, second_arg, (((0,), (0,)), ((), ())), preferred_element_type=F32
    )


def contract_cols(first_arg, second_arg):
    return lax.dot_general(
        first_arg, second_arg, (((1,), (1,)), ((), ())), preferred_element_type=F32
    )


def frame_row(row, lat_size):
    place = row + MARGIN
    return place // WLON * BAND + place % WLON * lat_size


def band_bias(lat_size):
    at = np.arange(BAND)
    group = np.where(at < WLON * lat_size, at % lat_size // WLAT, -1)
    return np.where(group[:, None] == group[None, :], 0.0, -1e30).astype(np.float32)


def merge_picks(lon_size, lat_size):
    picks = np.zeros((4, PAD, FRAME), np.float32)
    for i in range(lon_size // 2):
        for j in range(lat_size // 2):
            for a in range(2):
                for b in range(2):
                    picks[2 * a + b, i * (lat_size // 2) + j,
                          frame_row(2 * i + a, lat_size) + 2 * j + b] = 1.0
    return picks


def norm_parts(values):
    average = jnp.mean(values, axis=-1, keepdims=True)
    centred = values - average
    scale = lax.rsqrt(jnp.mean(centred * centred, axis=-1, keepdims=True) + EPSILON)
    return centred * scale, scale


def norm_back(unit, scale, grads):
    mean_grad = jnp.mean(grads, axis=-1, keepdims=True)
    mean_unit = jnp.mean(grads * unit, axis=-1, keepdims=True)
    return scale * (grads - mean_grad - unit * mean_unit)


def call(kernel, outs, scratch, flops, moved, *operands):
    return pl.pallas_call(
        kernel,
        out_shape=outs,
        scratch_shapes=scratch,
        compiler_params=pltpu.CompilerParams(vmem_limit_bytes=40 * 1024 * 1024),
        cost_estimate=pl.CostEstimate(flops=flops, transcendentals=0, bytes_accessed=moved),
    )(*operands)


def head_masks():
    lane = lax.broadcasted_iota(jnp.int32, (1, 128), 1)
    return lane < 64, lane >= 64


def softmax_rows(scores):
    top = jnp.max(scores, axis=-1, keepdims=True)
    raised = jnp.exp(scores - top)
    return raised / jnp.sum(raised, axis=-1, keepdims=True)


def forward_kernel(west, field, east, bias, picks, qkv_w, out_w, gain_f, gain_m,
                   merged, rows, mixed, heads, frame, xs):
    lon_size, lat_size, channels = field.shape
    xs[...] = jnp.zeros_like(xs)
    for row in range(-MARGIN, lon_size + MARGIN):
        at = frame_row(row, lat_size)
        if row < 0:
            part = west[row + MARGIN]
        elif row < lon_size:
            part = field[row]
        else:
            part = east[row - lon_size]
        xs[at : at + lat_size, :] = part.astype(F32)
    values = xs[...]
    frame[...] = values.astype(BF)
    unit, _ = norm_parts(values)
    normed = (unit * gain_f[...]).astype(BF)
    mixed[...] = jnp.dot(normed, qkv_w[...], preferred_element_type=F32).astype(BF)
    masks = head_masks()
    scale = 1.0 / math.sqrt(channels // HEADS)
    for band in range(2):
        span = pl.ds(band * BAND, BAND)
        for pair in range(HEADS // 2):
            query = mixed[span, pair * 128 : (pair + 1) * 128]
            key = mixed[span, channels + pair * 128 : channels + (pair + 1) * 128]
            value = mixed[span, 2 * channels + pair * 128 : 2 * channels + (pair + 1) * 128]
            got = []
            for mask in masks:
                scores = contract_cols(jnp.where(mask, query, 0), key) * scale + bias[...]
                weights = softmax_rows(scores).astype(BF)
                got.append(jnp.dot(weights, value, preferred_element_type=F32))
            heads[span, pair * 128 : (pair + 1) * 128] = jnp.where(
                masks[0], got[0], got[1]
            ).astype(BF)
    attended = jnp.dot(heads[...], out_w[...], preferred_element_type=F32)
    field_out = (values + attended).astype(BF)
    for part in range(4):
        rows[:, part * channels : (part + 1) * channels] = jnp.dot(
            picks[part], field_out, preferred_element_type=F32
        ).astype(BF)
    unit, _ = norm_parts(rows[...].astype(F32))
    merged[...] = (unit * gain_m[...]).astype(BF)


def merge_back_kernel(rows, cot, back, back_up, back_down, gain_m, picks, d_frame, to_east, to_west, grad_gain):
    channels = d_frame.shape[1]
    unit, scale = norm_parts(rows[...].astype(F32))
    d_merged = cot[...].astype(F32) + (
        back[...].astype(F32) + back_up[...].astype(F32) + back_down[...].astype(F32)
    )
    grad_gain[...] = jnp.sum(d_merged * unit, axis=0, keepdims=True)
    d_rows = norm_back(unit, scale, d_merged * gain_m[...])
    high = d_rows.astype(BF)
    low = (d_rows - high.astype(F32)).astype(BF)
    total = jnp.zeros(d_frame.shape, F32)
    for part in range(4):
        cols = slice(part * channels, (part + 1) * channels)
        total += contract_rows(picks[part], high[:, cols])
        total += contract_rows(picks[part], low[:, cols])
    d_frame[...] = total
    span = to_east.shape[0]
    to_west[...] = d_frame[span : 2 * span, :].astype(BF)
    to_east[...] = d_frame[BAND : BAND + span, :].astype(BF)


def backward_kernel(frame, mixed, heads, d_frame, d_west, d_east, bias, qkv_w, out_w, gain_f,
                    gain_grad_m, grad_field, grads, dfl, d_mixed):
    lon_size, lat_size, channels = grad_field.shape
    span_rows = d_west.shape[0]
    dfl[...] = d_frame[...]
    dfl[0:span_rows, :] = d_west[...].astype(F32)
    dfl[BAND + span_rows : BAND + 2 * span_rows, :] = d_east[...].astype(F32)
    d_flat = dfl[...].astype(BF)
    d_heads = contract_cols(d_flat, out_w[...]).astype(BF)
    grad_out = contract_rows(heads[:BAND, :], d_flat[:BAND, :]).astype(BF)
    masks = head_masks()
    factor = 1.0 / math.sqrt(channels // HEADS)
    for band in range(2):
        span = pl.ds(band * BAND, BAND)
        for pair in range(HEADS // 2):
            cols = [slice(k * channels + pair * 128, k * channels + (pair + 1) * 128)
                    for k in range(3)]
            query, key, value = (mixed[span, c] for c in cols)
            d_out = d_heads[band * BAND : (band + 1) * BAND, cols[0]]
            got = []
            for mask in masks:
                own_query = jnp.where(mask, query, 0)
                scores = contract_cols(own_query, key) * factor + bias[...]
                weights = softmax_rows(scores)
                d_own = jnp.where(mask, d_out, 0)
                d_weights = contract_cols(d_own, value).astype(BF).astype(F32)
                d_value = contract_rows(weights.astype(BF), d_own)
                inner = jnp.sum(d_weights * weights, axis=-1, keepdims=True)
                d_scores = (weights * (d_weights - inner) * factor).astype(BF)
                d_query = jnp.dot(d_scores, key, preferred_element_type=F32)
                d_key = contract_rows(d_scores, own_query)
                got.append((d_query, d_key, d_value))
            for c, first, second in zip(cols, *got):
                d_mixed[span, c] = jnp.where(masks[0], first, second).astype(BF)
    unit, scale = norm_parts(frame[...].astype(F32))
    normed = (unit * gain_f[...]).astype(BF)
    grad_qkv = contract_rows(normed[:BAND, :], d_mixed[:BAND, :]).astype(BF)
    d_normed = contract_cols(d_mixed[...], qkv_w[...])
    grad_gain = jnp.sum(d_normed[:BAND, :] * unit[:BAND, :], axis=0, keepdims=True)
    dfl[...] = d_frame[...] + norm_back(unit, scale, d_normed * gain_f[...])
    for row in range(lon_size):
        at = frame_row(row, lat_size)
        grad_field[row] = dfl[at : at + lat_size, :]
    half = channels // 2
    top = lax.broadcasted_iota(jnp.int32, (16, 128), 0) == 0
    for core in range(2):
        own = slice(core * half, (core + 1) * half)
        for k in range(16):
            if k < 12:
                block = grad_qkv[own, k * 128 : (k + 1) * 128]
            else:
                block = grad_out[own, (k - 12) * 128 : (k - 11) * 128]
            grads[core, k, 0:half, :] = block
            if core == 0:
                gain = gain_grad_m[:, k * 128 : (k + 1) * 128]
            elif k < 4:
                gain = grad_gain[:, k * 128 : (k + 1) * 128]
            else:
                gain = jnp.zeros((1, 128), F32)
            grads[core, k, half : half + 16, :] = jnp.where(top, gain, 0.0).astype(BF)


def add_up_kernel(terms, total):
    acc = terms[0].astype(F32)
    for k in range(1, terms.shape[0]):
        acc += terms[k].astype(F32)
    total[...] = acc.astype(total.dtype)


def spread_kernel(core, mine, other, grad_qkv, grad_out, gain_f, gain_m):
    half = grad_out.shape[0] // 2
    for whose, part in ((core[0], mine), (1 - core[0], other)):
        own = pl.ds(pl.multiple_of(whose * half, half), half)
        for k in range(16):
            block = part[k, 0:half, :].astype(F32)
            if k < 12:
                grad_qkv[own, k * 128 : (k + 1) * 128] = block
            else:
                grad_out[own, (k - 12) * 128 : (k - 11) * 128] = block
    for k in range(16):
        pair = mine[k, half : half + 16, :].astype(F32), other[k, half : half + 16, :].astype(F32)
        first = jnp.where(core[0] == 0, pair[0], pair[1])
        gain_m[:, k * 128 : (k + 1) * 128] = first[0:1, :]
        if k < 4:
            second = jnp.where(core[0] == 0, pair[1], pair[0])
            gain_f[:, k * 128 : (k + 1) * 128] = second[0:1, :]


def shape(*size, of=BF):
    return jax.ShapeDtypeStruct(size, of)


def share_weights(part, core):
    half = part.shape[0] // 2
    mine = lax.dynamic_slice_in_dim(part, core * half, half, 0)
    mine = swap(mine, "xl")
    other = swap(mine, "c")
    first = jnp.where(core == 0, mine, other)
    second = jnp.where(core == 0, other, mine)
    return jnp.concatenate([first, second], axis=0)


def sum_over_mesh(grads, core):
    keep = lax.dynamic_index_in_dim(grads, core, 0, keepdims=False)
    give = lax.dynamic_index_in_dim(grads, 1 - core, 0, keepdims=False)
    size = keep.shape
    total = (keep.astype(F32) + swap(give, "c").astype(F32)).astype(BF)
    total = lax.all_to_all(total, PLANE, split_axis=0, concat_axis=0, tiled=True)
    total = call(add_up_kernel, shape(*size[1:]), [], 2 * 10**6, 2 * 10**6, total)
    for bit in (1, 2, 4):
        total = (total.astype(F32) + swap(total, "z", bit).astype(F32)).astype(BF)
    total = jnp.broadcast_to(total, size)
    mine = lax.all_to_all(total, PLANE, split_axis=0, concat_axis=0, tiled=True)
    return mine, swap(mine, "c")


def on_device(
    fine_field, qkv_weight, out_weight, gain_fine, gain_merge, up_weight, down_weight, cotangent
):
    core = lax.axis_index("c")
    lon_size, lat_size, channels = fine_field.shape
    west = shift(fine_field[lon_size - MARGIN :], LON, 1)
    east = shift(fine_field[:MARGIN], LON, -1)

    grad_rows = cotangent.reshape(-1, 4 * channels)
    tokens = grad_rows.shape[0]
    grad_rows = jnp.pad(grad_rows, ((0, PAD - tokens), (0, 0)))
    grad_all = lax.all_gather(grad_rows, "z", axis=0)
    place = lax.axis_index("z")
    grad_all = jnp.concatenate(
        [lax.dynamic_index_in_dim(grad_all, (place + k) % 8, 0, keepdims=False) for k in range(8)]
    )

    up_weight, down_weight, west, east = lax.optimization_barrier(
        (up_weight, down_weight, west, east)
    )
    up_both = jnp.concatenate([up_weight, share_weights(up_weight, core)], axis=1)
    down_both = jnp.concatenate([down_weight, share_weights(down_weight, core)], axis=0)

    bias = jnp.asarray(band_bias(lat_size))
    picks = jnp.asarray(merge_picks(lon_size, lat_size), BF)
    gain_f = gain_fine.reshape(1, -1)
    gain_m = gain_merge.reshape(1, -1)
    merged, rows, mixed, heads, frame = call(
        forward_kernel,
        (shape(PAD, 4 * channels), shape(PAD, 4 * channels), shape(FRAME, 3 * channels),
         shape(FRAME, channels), shape(FRAME, channels)),
        [pltpu.VMEM((FRAME, channels), F32)],
        10**10, 8 * 10**6,
        west, fine_field, east, bias, picks, qkv_weight, out_weight, gain_f, gain_m,
    )
    merged_all = jnp.concatenate(gather_around(merged, "z"))

    pre_act = jnp.dot(merged_all, up_both, preferred_element_type=F32)
    activation, gelu_pull = jax.vjp(jax.nn.gelu, pre_act)
    act_low = activation.astype(BF)
    d_act = contract_cols(grad_all, down_both)
    d_pre = gelu_pull(d_act)[0].astype(BF)
    back_term = contract_cols(d_pre, up_both).astype(BF)
    back_up, back_down = scatter_around(
        [back_term[k * PAD : (k + 1) * PAD] for k in range(8)], "z"
    )
    act_low, back_term = lax.optimization_barrier((act_low, back_term))
    block_term = jnp.dot(act_low, down_both, preferred_element_type=F32).astype(BF)
    block_term = jnp.concatenate(
        [lax.dynamic_slice_in_dim(block_term, (k - place) % 8 * PAD, PAD, 0) for k in range(8)]
    )
    summed = lax.psum_scatter(block_term, "z", scatter_dimension=0, tiled=True)
    bottleneck = (
        (merged[:tokens].astype(F32) + summed[:tokens].astype(F32))
        .astype(BF)
        .reshape(cotangent.shape)
    )

    hidden = up_weight.shape[1]

    def sum_columns(grads):
        cut = grads.astype(BF).reshape(8, 2, -1, 2 * hidden)
        keep = lax.dynamic_index_in_dim(cut, core, 1, keepdims=False)
        give = lax.dynamic_index_in_dim(cut, 1 - core, 1, keepdims=False)
        pair = add_low(keep, swap(give, "c"))
        pair = add_low(pair[:, :, :hidden], swap(pair[:, :, hidden:], "xl"))
        terms = lax.all_to_all(pair, ("y", "xh"), split_axis=0, concat_axis=0, tiled=True)
        return call(add_up_kernel, shape(*pair.shape[1:], of=F32), [], 10**6, 10**6, terms)

    grad_up_part = sum_columns(contract_rows(merged_all, d_pre))
    grad_down_part = sum_columns(contract_rows(grad_all, act_low)).T

    edge = MARGIN * lat_size
    d_frame, to_east, to_west, gain_grad_m = call(
        merge_back_kernel,
        (shape(FRAME, channels, of=F32), shape(edge, channels), shape(edge, channels),
         shape(1, 4 * channels, of=F32)),
        [],
        10**9, 2 * 10**6,
        rows, grad_rows, back_term[:PAD], back_up, back_down, gain_m, picks,
    )
    d_west = shift(to_east, LON, 1)
    d_east = shift(to_west, LON, -1)
    grad_field, grads = call(
        backward_kernel,
        (shape(lon_size, lat_size, channels, of=F32), shape(2, 16, channels // 2 + 16, 128)),
        [pltpu.VMEM((FRAME, channels), F32), pltpu.VMEM((FRAME, 3 * channels), BF)],
        2 * 10**10, 10**7,
        frame, mixed, heads, d_frame, d_west, d_east, bias, qkv_weight, out_weight, gain_f,
        gain_grad_m,
    )
    mine, other = sum_over_mesh(grads, core)
    whole = pl.BlockSpec(memory_space=pltpu.VMEM)
    grad_qkv, grad_out, grad_gain_fine, grad_gain_merge = pl.pallas_call(
        spread_kernel,
        out_shape=(shape(channels, 3 * channels, of=F32), shape(channels, channels, of=F32),
                   shape(1, channels, of=F32), shape(1, 4 * channels, of=F32)),
        in_specs=[pl.BlockSpec(memory_space=pltpu.SMEM), whole, whole],
        compiler_params=pltpu.CompilerParams(vmem_limit_bytes=40 * 1024 * 1024),
    )(core.reshape(1), mine, other)
    return (
        bottleneck,
        grad_field,
        grad_qkv,
        grad_out,
        grad_gain_fine.reshape(-1),
        grad_gain_merge.reshape(-1),
        grad_up_part,
        grad_down_part,
    )


def solution(mesh):
    torus = Mesh(mesh.devices.reshape(4, 2, 2, 8, 2), LON + LAT)
    placed = (
        P(LON, LAT, None),
        P(),
        P(),
        P(),
        P(),
        P(None, LAT),
        P(LAT, None),
        P(LON, LAT, None),
    )
    return jax.shard_map(
        on_device,
        mesh=torus,
        in_specs=placed,
        out_specs=(
            P(LON, LAT, None),
            P(LON, LAT, None),
            P(),
            P(),
            P(),
            P(),
            P(LON, LAT),
            P(LAT, LON),
        ),
        check_vma=False,
    )
```

```python
import math

import jax
import jax.numpy as jnp
import numpy as np
from jax import lax
from jax.experimental import pallas as pl
from jax.experimental.pallas import tpu as pltpu
from jax.sharding import Mesh
from jax.sharding import PartitionSpec as P

HEADS = 8
WLON = 12
WLAT = 6
MARGIN = WLON // 2
EPSILON = 1e-05
LON = ("y", "xh", "c")
LAT = ("z", "xl")
PLANE = ("y", "xh", "xl")
BF = jnp.bfloat16
F32 = jnp.float32
PAD = 56
SLOT = 64
BAND = 224
FRAME = 2 * BAND


def shift(block, axis, distance):
    size = lax.axis_size(axis)
    return lax.ppermute(block, axis, [(i, (i + distance) % size) for i in range(size)])


def swap(block, axis, bit=1):
    size = lax.axis_size(axis)
    return lax.ppermute(block, axis, [(i, i ^ bit) for i in range(size)])


def add_low(first_arg, second_arg):
    return (first_arg.astype(F32) + second_arg.astype(F32)).astype(BF)


def gather_around(block, axis, fillers):
    size = lax.axis_size(axis)
    half = size // 2
    width = block.shape[1] // 2
    got = {0: block}
    behind = ahead = block
    done = []
    for step in range(1, half + 1):
        if step == half:
            behind, ahead = behind[:, :width], ahead[:, width:]
        behind = shift(behind, axis, 1)
        ahead = shift(ahead, axis, -1)
        behind, ahead, extra = lax.optimization_barrier(
            (behind, ahead, fillers[step - 1](*done))
        )
        done.append(extra)
        got[size - step] = behind
        got[step] = ahead
    got[half] = jnp.concatenate([behind, ahead], axis=1)
    return [got[k] for k in range(size)], done


def scatter_around(terms, axis, fillers):
    size = lax.axis_size(axis)
    half = size // 2
    width = terms[0].shape[1] // 2

    def step(first, second, filler):
        first = shift(first, axis, 1)
        second = shift(second, axis, -1)
        return lax.optimization_barrier((first, second, filler()))

    up, down, got = step(terms[half][:, :width], terms[half][:, width:], fillers[0])
    done = [got]
    up = jnp.concatenate([add_low(terms[half - 1][:, :width], up), terms[half - 1][:, width:]], 1)
    down = jnp.concatenate(
        [terms[half + 1][:, :width], add_low(terms[half + 1][:, width:], down)], 1
    )
    for ahead in range(half - 2, -1, -1):
        up, down, got = step(up, down, lambda: fillers[half - 1 - ahead](*done))
        done.append(got)
        if ahead:
            up = add_low(terms[ahead], up)
            down = add_low(terms[size - ahead], down)
    return up, down, done


def contract_rows(first_arg, second_arg):
    return lax.dot_general(
        first_arg, second_arg, (((0,), (0,)), ((), ())), preferred_element_type=F32
    )


def contract_cols(first_arg, second_arg):
    return lax.dot_general(
        first_arg, second_arg, (((1,), (1,)), ((), ())), preferred_element_type=F32
    )


def frame_row(row, lat_size):
    place = row + MARGIN
    return place // WLON * BAND + place % WLON * lat_size


def band_bias(lat_size):
    at = np.arange(BAND)
    group = np.where(at < WLON * lat_size, at % lat_size // WLAT, -1)
    return np.where(group[:, None] == group[None, :], 0.0, -1e30).astype(np.float32)


def merge_picks(lon_size, lat_size):
    picks = np.zeros((4, PAD, FRAME), np.float32)
    for i in range(lon_size // 2):
        for j in range(lat_size // 2):
            for a in range(2):
                for b in range(2):
                    picks[2 * a + b, i * (lat_size // 2) + j,
                          frame_row(2 * i + a, lat_size) + 2 * j + b] = 1.0
    return picks


def norm_parts(values):
    average = jnp.mean(values, axis=-1, keepdims=True)
    centred = values - average
    scale = lax.rsqrt(jnp.mean(centred * centred, axis=-1, keepdims=True) + EPSILON)
    return centred * scale, scale


def norm_back(unit, scale, grads):
    mean_grad = jnp.mean(grads, axis=-1, keepdims=True)
    mean_unit = jnp.mean(grads * unit, axis=-1, keepdims=True)
    return scale * (grads - mean_grad - unit * mean_unit)


def call(kernel, outs, scratch, flops, moved, *operands):
    spaces = [
        pltpu.SMEM if operand.dtype == jnp.int32 else pltpu.VMEM for operand in operands
    ]
    return pl.pallas_call(
        kernel,
        out_shape=outs,
        in_specs=[pl.BlockSpec(memory_space=space) for space in spaces],
        scratch_shapes=scratch,
        compiler_params=pltpu.CompilerParams(vmem_limit_bytes=20 * 1024 * 1024),
        cost_estimate=pl.CostEstimate(flops=flops, transcendentals=0, bytes_accessed=moved),
    )(*operands)


def head_masks():
    lane = lax.broadcasted_iota(jnp.int32, (1, 128), 1)
    return lane < 64, lane >= 64


def softmax_rows(scores):
    top = jnp.max(scores, axis=-1, keepdims=True)
    raised = jnp.exp(scores - top)
    return raised / jnp.sum(raised, axis=-1, keepdims=True)


def forward_kernel(west, field, east, bias, picks, qkv_w, out_w, gain_f, gain_m,
                   merged, rows, mixed, heads, frame, xs):
    lon_size, lat_size, channels = field.shape
    xs[...] = jnp.zeros_like(xs)
    for row in range(-MARGIN, lon_size + MARGIN):
        at = frame_row(row, lat_size)
        if row < 0:
            part = west[row + MARGIN]
        elif row < lon_size:
            part = field[row]
        else:
            part = east[row - lon_size]
        xs[at : at + lat_size, :] = part.astype(F32)
    values = xs[...]
    frame[...] = values.astype(BF)
    unit, _ = norm_parts(values)
    normed = (unit * gain_f[...]).astype(BF)
    mixed[...] = jnp.dot(normed, qkv_w[...], preferred_element_type=F32).astype(BF)
    masks = head_masks()
    scale = 1.0 / math.sqrt(channels // HEADS)
    for band in range(2):
        span = pl.ds(band * BAND, BAND)
        for pair in range(HEADS // 2):
            query = mixed[span, pair * 128 : (pair + 1) * 128]
            key = mixed[span, channels + pair * 128 : channels + (pair + 1) * 128]
            value = mixed[span, 2 * channels + pair * 128 : 2 * channels + (pair + 1) * 128]
            got = []
            for mask in masks:
                scores = contract_cols(jnp.where(mask, query, 0), key) * scale + bias[...]
                weights = softmax_rows(scores).astype(BF)
                got.append(jnp.dot(weights, value, preferred_element_type=F32))
            heads[span, pair * 128 : (pair + 1) * 128] = jnp.where(
                masks[0], got[0], got[1]
            ).astype(BF)
    attended = jnp.dot(heads[...], out_w[...], preferred_element_type=F32)
    field_out = (values + attended).astype(BF)
    for part in range(4):
        rows[:, part * channels : (part + 1) * channels] = jnp.dot(
            picks[part], field_out, preferred_element_type=F32
        ).astype(BF)
    unit, _ = norm_parts(rows[...].astype(F32))
    merged[...] = (unit * gain_m[...]).astype(BF)


def merge_back_kernel(rows, cot, back, back_up, back_down, gain_m, picks, d_frame, to_east, to_west, grad_gain):
    channels = d_frame.shape[1]
    unit, scale = norm_parts(rows[...].astype(F32))
    d_merged = cot[...].astype(F32) + (
        back[...].astype(F32) + back_up[...].astype(F32) + back_down[...].astype(F32)
    )
    grad_gain[...] = jnp.sum(d_merged * unit, axis=0, keepdims=True)
    d_rows = norm_back(unit, scale, d_merged * gain_m[...])
    high = d_rows.astype(BF)
    low = (d_rows - high.astype(F32)).astype(BF)
    total = jnp.zeros(d_frame.shape, F32)
    for part in range(4):
        cols = slice(part * channels, (part + 1) * channels)
        total += contract_rows(picks[part], high[:, cols])
        total += contract_rows(picks[part], low[:, cols])
    d_frame[...] = total
    span = to_east.shape[0]
    to_west[...] = d_frame[span : 2 * span, :].astype(BF)
    to_east[...] = d_frame[BAND : BAND + span, :].astype(BF)


def backward_kernel(core, frame, mixed, heads, d_frame, d_west, d_east, bias, qkv_w, out_w, gain_f,
                    gain_grad_m, grad_field, keep, give, dfl, d_mixed):
    lon_size, lat_size, channels = grad_field.shape
    span_rows = d_west.shape[0]
    dfl[...] = d_frame[...]
    dfl[0:span_rows, :] = d_west[...].astype(F32)
    dfl[BAND + span_rows : BAND + 2 * span_rows, :] = d_east[...].astype(F32)
    d_flat = dfl[...].astype(BF)
    d_heads = contract_cols(d_flat, out_w[...]).astype(BF)
    grad_out = contract_rows(heads[:BAND, :], d_flat[:BAND, :]).astype(BF)
    masks = head_masks()
    factor = 1.0 / math.sqrt(channels // HEADS)
    for band in range(2):
        span = pl.ds(band * BAND, BAND)
        for pair in range(HEADS // 2):
            cols = [slice(k * channels + pair * 128, k * channels + (pair + 1) * 128)
                    for k in range(3)]
            query, key, value = (mixed[span, c] for c in cols)
            d_out = d_heads[band * BAND : (band + 1) * BAND, cols[0]]
            got = []
            for mask in masks:
                own_query = jnp.where(mask, query, 0)
                scores = contract_cols(own_query, key) * factor + bias[...]
                weights = softmax_rows(scores)
                d_own = jnp.where(mask, d_out, 0)
                d_weights = contract_cols(d_own, value).astype(BF).astype(F32)
                d_value = contract_rows(weights.astype(BF), d_own)
                inner = jnp.sum(d_weights * weights, axis=-1, keepdims=True)
                d_scores = (weights * (d_weights - inner) * factor).astype(BF)
                d_query = jnp.dot(d_scores, key, preferred_element_type=F32)
                d_key = contract_rows(d_scores, own_query)
                got.append((d_query, d_key, d_value))
            for c, first, second in zip(cols, *got):
                d_mixed[span, c] = jnp.where(masks[0], first, second).astype(BF)
    unit, scale = norm_parts(frame[...].astype(F32))
    normed = (unit * gain_f[...]).astype(BF)
    grad_qkv = contract_rows(normed[:BAND, :], d_mixed[:BAND, :]).astype(BF)
    d_normed = contract_cols(d_mixed[...], qkv_w[...])
    grad_gain = jnp.sum(d_normed[:BAND, :] * unit[:BAND, :], axis=0, keepdims=True)
    dfl[...] = d_frame[...] + norm_back(unit, scale, d_normed * gain_f[...])
    for row in range(lon_size):
        at = frame_row(row, lat_size)
        grad_field[row] = dfl[at : at + lat_size, :]
    half = channels // 2
    top = lax.broadcasted_iota(jnp.int32, (16, 128), 0) == 0
    first = core[0] == 0
    for k in range(16):
        source, at = (grad_qkv, k) if k < 12 else (grad_out, k - 12)
        low = source[:half, at * 128 : (at + 1) * 128]
        high = source[half:, at * 128 : (at + 1) * 128]
        keep[k, 0:half, :] = jnp.where(first, low, high)
        give[k, 0:half, :] = jnp.where(first, high, low)
        low = jnp.where(top, gain_grad_m[:, k * 128 : (k + 1) * 128], 0.0)
        high = jnp.where(top, grad_gain[:, k * 128 : (k + 1) * 128], 0.0) if k < 4 else 0.0 * low
        keep[k, half : half + 16, :] = jnp.where(first, low, high).astype(BF)
        give[k, half : half + 16, :] = jnp.where(first, high, low).astype(BF)


def add_up_kernel(terms, total):
    acc = terms[0].astype(F32)
    for k in range(1, terms.shape[0]):
        acc += terms[k].astype(F32)
    total[...] = acc.astype(total.dtype)


def spread_kernel(core, mine, other, grad_qkv, grad_out, gain_f, gain_m):
    half = grad_out.shape[0] // 2
    for whose, part in ((core[0], mine), (1 - core[0], other)):
        own = pl.ds(pl.multiple_of(whose * half, half), half)
        for k in range(16):
            block = part[k, 0:half, :].astype(F32)
            if k < 12:
                grad_qkv[own, k * 128 : (k + 1) * 128] = block
            else:
                grad_out[own, (k - 12) * 128 : (k - 11) * 128] = block
    for k in range(16):
        pair = mine[k, half : half + 16, :].astype(F32), other[k, half : half + 16, :].astype(F32)
        first = jnp.where(core[0] == 0, pair[0], pair[1])
        gain_m[:, k * 128 : (k + 1) * 128] = first[0:1, :]
        if k < 4:
            second = jnp.where(core[0] == 0, pair[1], pair[0])
            gain_f[:, k * 128 : (k + 1) * 128] = second[0:1, :]


def stack_chunks(chunks, whole):
    gap = jnp.zeros((SLOT - PAD, whole.shape[1]), F32)
    for k, chunk in enumerate(chunks):
        filled = jnp.concatenate([chunk[...].astype(F32), gap], axis=0)
        whole[k * SLOT : (k + 1) * SLOT, :] = filled.astype(BF)


def join_halves(core, mine, other, whole):
    half = mine.shape[0]
    whole[pl.ds(pl.multiple_of(core * half, half), half), :] = mine[...]
    whole[pl.ds(pl.multiple_of((1 - core) * half, half), half), :] = other[...]


def gelu_parts(pre):
    slope = math.sqrt(2.0 / math.pi)
    square = pre * pre
    bent = jnp.tanh(slope * (pre + 0.044715 * square * pre))
    value = 0.5 * pre * (1.0 + bent)
    rate = slope * (1.0 + 3 * 0.044715 * square)
    return value, 0.5 * (1.0 + bent) + 0.5 * pre * (1.0 - bent * bent) * rate


def act_grad_kernel(place, core, chunks, own, mine, other, cot_all, d_act, shared):
    stack_chunks([chunks.at[lax.rem(place[0] + k, 8)] for k in range(8)], cot_all)
    join_halves(core[0], mine, other, shared)
    hidden = own.shape[0]
    for k, weight in enumerate((own, shared)):
        d_act[:, k * hidden : (k + 1) * hidden] = contract_cols(cot_all[...], weight[...])


def mlp_kernel(core, *refs):
    chunks, refs = refs[:8], refs[8:]
    (d_act, own, mine, other), refs = refs[:4], refs[4:]
    (merged_all, act, d_pre), refs = refs[:3], refs[3:]
    backs, (shared,) = refs[:8], refs[8:]
    stack_chunks(chunks, merged_all)
    join_halves(core[0], mine, other, shared)
    hidden = own.shape[1]
    for k, weight in enumerate((own, shared)):
        for at in range(0, hidden, 256):
            cols = slice(k * hidden + at, k * hidden + at + 256)
            pre = jnp.dot(merged_all[...], weight[:, at : at + 256], preferred_element_type=F32)
            value, slope = gelu_parts(pre)
            act[:, cols] = value.astype(BF)
            d_pre[:, cols] = (d_act[:, cols] * slope).astype(BF)
    for at in range(0, own.shape[0], 256):
        cols = slice(at, at + 256)
        term = contract_cols(d_pre[:, :hidden], own[cols, :])
        term += contract_cols(d_pre[:, hidden:], shared[cols, :])
        for k in range(8):
            backs[k][:, cols] = term[k * SLOT : k * SLOT + PAD, :].astype(BF)


def block_kernel(place, core, act, own, mine, other, terms, shared):
    join_halves(core[0], mine, other, shared)
    hidden = own.shape[0]
    for at in range(0, own.shape[1], 256):
        cols = slice(at, at + 256)
        term = jnp.dot(act[:, :hidden], own[:, cols], preferred_element_type=F32)
        term += jnp.dot(act[:, hidden:], shared[:, cols], preferred_element_type=F32)
        for k in range(8):
            terms[lax.rem(place[0] + k, 8), :, cols] = (
                term[k * SLOT : k * SLOT + PAD, :].astype(BF)
            )


def weight_grad_kernel(core, tokens, hidden, keep, give):
    for k in range(keep.shape[0]):
        both = contract_rows(tokens[:, k * 256 : (k + 1) * 256], hidden[...]).astype(BF)
        low, high = both[:128, :], both[128:, :]
        keep[k] = jnp.where(core[0] == 0, low, high)
        give[k] = jnp.where(core[0] == 0, high, low)


def shape(*size, of=BF):
    return jax.ShapeDtypeStruct(size, of)


def on_device(
    fine_field, qkv_weight, out_weight, gain_fine, gain_merge, up_weight, down_weight, cotangent
):
    core = lax.axis_index("c")
    whose = core.reshape(1)
    place = lax.axis_index("z").reshape(1)
    lon_size, lat_size, channels = fine_field.shape
    west = shift(fine_field[lon_size - MARGIN :], LON, 1)
    east = shift(fine_field[:MARGIN], LON, -1)

    grad_rows = cotangent.reshape(-1, 4 * channels)
    tokens = grad_rows.shape[0]
    grad_rows = jnp.pad(grad_rows, ((0, PAD - tokens), (0, 0)))
    grad_chunks = lax.all_gather(grad_rows, "z", axis=0)
    hidden = up_weight.shape[1]
    slots = 8 * SLOT

    halves = [part.shape[0] // 2 for part in (down_weight, up_weight)]
    west, east, down_mine, up_mine = lax.optimization_barrier((
        west,
        east,
        lax.dynamic_slice_in_dim(down_weight, core * halves[0], halves[0], 0),
        lax.dynamic_slice_in_dim(up_weight, core * halves[1], halves[1], 0),
    ))
    down_mine = swap(down_mine, "xl")
    up_mine = swap(up_mine, "xl")

    def act_grads(down_pair):
        return call(
            act_grad_kernel,
            (shape(slots, 4 * channels), shape(slots, 2 * hidden, of=F32)),
            [pltpu.VMEM((hidden, 4 * channels), BF)],
            2 * 10**9, 10**7,
            place, whose, grad_chunks, down_weight, *down_pair,
        )

    bias = jnp.asarray(band_bias(lat_size))
    picks = jnp.asarray(merge_picks(lon_size, lat_size), BF)
    gain_f = gain_fine.reshape(1, -1)
    gain_m = gain_merge.reshape(1, -1)
    merged, rows, mixed, heads, frame = call(
        forward_kernel,
        (shape(PAD, 4 * channels), shape(PAD, 4 * channels), shape(FRAME, 3 * channels),
         shape(FRAME, channels), shape(FRAME, channels)),
        [pltpu.VMEM((FRAME, channels), F32)],
        10**10, 8 * 10**6,
        west, fine_field, east, bias, picks, qkv_weight, out_weight, gain_f, gain_m,
    )
    merged_chunks, done = gather_around(
        merged,
        "z",
        [
            lambda: (),
            lambda first: down_mine,
            lambda first, second: (second, swap(second, "c"), up_mine),
            lambda first, second, third: (act_grads(third[:2]), swap(third[2], "c")),
        ],
    )
    down_mine, down_other, up_mine = done[2]
    (cot_all, d_act), up_other = done[3]
    merged_all, act, d_pre, *backs = call(
        mlp_kernel,
        (shape(slots, 4 * channels), shape(slots, 2 * hidden), shape(slots, 2 * hidden),
         *[shape(PAD, 4 * channels)] * 8),
        [pltpu.VMEM((4 * channels, hidden), BF)],
        5 * 10**9, 10**7,
        whose, *merged_chunks, d_act, up_weight, up_mine, up_other,
    )

    def weight_grad(rows, columns):
        keep, give = call(
            weight_grad_kernel,
            (shape(8, 128, 2 * hidden), shape(8, 128, 2 * hidden)),
            [],
            2 * 10**9, 10**7,
            whose, rows, columns,
        )
        return keep, give

    def far_half(pair):
        return add_low(pair[0][:, :, hidden:], pair[1][:, :, hidden:])

    def near_half(pair, far):
        near = pair[0][:, :, :hidden].astype(F32) + pair[1][:, :, :hidden].astype(F32)
        return (near + far.astype(F32)).astype(BF)

    def over_plane(pair):
        return lax.all_to_all(pair, ("y", "xh"), split_axis=0, concat_axis=0, tiled=True)

    def add_plane(terms):
        return call(add_up_kernel, shape(*terms.shape[1:], of=F32), [], 10**6, 10**6, terms)

    def block_terms():
        return call(
            block_kernel,
            shape(8, PAD, 4 * channels),
            [pltpu.VMEM((hidden, 4 * channels), BF)],
            2 * 10**9, 10**7,
            place, whose, act, down_weight, down_mine, down_other,
        )

    back_up, back_down, done = scatter_around(
        backs,
        "z",
        [
            lambda: weight_grad(merged_all, d_pre),
            lambda up: (weight_grad(cot_all, act), swap(up[1], "c")),
            lambda up, mid: (
                swap(mid[0][1], "c"),
                far_half((up[0], mid[1])),
                block_terms(),
            ),
            lambda up, mid, late: far_half((mid[0][0], late[0])),
        ],
    )
    up_pair = done[0][0], done[1][1]
    down_pair = done[1][0][0], done[2][0]
    up_far, terms = done[2][1:]
    down_far = done[3]
    up_far = swap(up_far, "xl")
    summed = lax.psum_scatter(
        terms.reshape(8 * PAD, 4 * channels), "z", scatter_dimension=0, tiled=True
    )

    edge = MARGIN * lat_size
    d_frame, to_east, to_west, gain_grad_m = call(
        merge_back_kernel,
        (shape(FRAME, channels, of=F32), shape(edge, channels), shape(edge, channels),
         shape(1, 4 * channels, of=F32)),
        [],
        10**9, 2 * 10**6,
        rows, grad_rows, backs[0], back_up, back_down, gain_m, picks,
    )
    d_west = shift(to_east, LON, 1)
    d_east = shift(to_west, LON, -1)
    d_west, d_east, down_far, up_near = lax.optimization_barrier(
        (d_west, d_east, down_far, near_half(up_pair, up_far))
    )
    down_far = swap(down_far, "xl")
    up_terms = over_plane(up_near)
    size = (16, channels // 2 + 16, 128)
    grad_field, keep, give = call(
        backward_kernel,
        (shape(lon_size, lat_size, channels, of=F32), shape(*size), shape(*size)),
        [pltpu.VMEM((FRAME, channels), F32), pltpu.VMEM((FRAME, 3 * channels), BF)],
        2 * 10**10, 10**7,
        whose, frame, mixed, heads, d_frame, d_west, d_east, bias, qkv_weight, out_weight, gain_f,
        gain_grad_m,
    )
    keep, give, up_terms = lax.optimization_barrier((keep, give, up_terms))
    total = add_low(keep, swap(give, "c"))
    total = lax.all_to_all(total, PLANE, split_axis=0, concat_axis=0, tiled=True)
    total, down_far, summed = lax.optimization_barrier((total, down_far, summed))
    down_terms = over_plane(near_half(down_pair, down_far))
    bottleneck = (
        (merged[:tokens].astype(F32) + summed[:tokens].astype(F32))
        .astype(BF)
        .reshape(cotangent.shape)
    )
    total = call(add_up_kernel, shape(*size[1:]), [], 2 * 10**6, 2 * 10**6, total)
    for bit in (1, 2, 4):
        total = add_low(total, swap(total, "z", bit))
    total, down_terms = lax.optimization_barrier((total, down_terms))
    total = jnp.broadcast_to(total, size)
    mine = lax.all_to_all(total, PLANE, split_axis=0, concat_axis=0, tiled=True)
    other = swap(mine, "c")
    grad_up_part = add_plane(up_terms)
    grad_down_part = add_plane(down_terms).T
    grad_qkv, grad_out, grad_gain_fine, grad_gain_merge = call(
        spread_kernel,
        (shape(channels, 3 * channels, of=F32), shape(channels, channels, of=F32),
         shape(1, channels, of=F32), shape(1, 4 * channels, of=F32)),
        [],
        10**6, 5 * 10**6,
        whose, mine, other,
    )
    return (
        bottleneck,
        grad_field,
        grad_qkv,
        grad_out,
        grad_gain_fine.reshape(-1),
        grad_gain_merge.reshape(-1),
        grad_up_part,
        grad_down_part,
    )


def solution(mesh):
    torus = Mesh(mesh.devices.reshape(4, 2, 2, 8, 2), LON + LAT)
    placed = (
        P(LON, LAT, None),
        P(),
        P(),
        P(),
        P(),
        P(None, LAT),
        P(LAT, None),
        P(LON, LAT, None),
    )
    return jax.shard_map(
        on_device,
        mesh=torus,
        in_specs=placed,
        out_specs=(
            P(LON, LAT, None),
            P(LON, LAT, None),
            P(),
            P(),
            P(),
            P(),
            P(LON, LAT),
            P(LAT, LON),
        ),
        check_vma=False,
    )
```

```python
import math

import jax
import jax.numpy as jnp
import numpy as np
from jax import lax
from jax.experimental import pallas as pl
from jax.experimental.pallas import tpu as pltpu
from jax.sharding import Mesh
from jax.sharding import PartitionSpec as P

HEADS = 8
WLON = 12
WLAT = 6
MARGIN = WLON // 2
EPSILON = 1e-05
LON = ("y", "xh", "c")
LAT = ("z", "xl")
PLANE = ("y", "xh", "xl")
BF = jnp.bfloat16
F32 = jnp.float32
PAD = 56
SLOT = 64
BAND = 224
FRAME = 2 * BAND


def shift(block, axis, distance):
    size = lax.axis_size(axis)
    return lax.ppermute(block, axis, [(i, (i + distance) % size) for i in range(size)])


def swap(block, axis, bit=1):
    size = lax.axis_size(axis)
    return lax.ppermute(block, axis, [(i, i ^ bit) for i in range(size)])


def add_low(first_arg, second_arg):
    return (first_arg.astype(F32) + second_arg.astype(F32)).astype(BF)


def gather_around(block, axis, fillers):
    size = lax.axis_size(axis)
    half = size // 2
    width = block.shape[1] // 2
    got = {0: block}
    behind = ahead = block
    done = []
    for step in range(1, half + 1):
        if step == half:
            behind, ahead = behind[:, :width], ahead[:, width:]
        behind = shift(behind, axis, 1)
        ahead = shift(ahead, axis, -1)
        behind, ahead, extra = lax.optimization_barrier(
            (behind, ahead, fillers[step - 1](*done))
        )
        done.append(extra)
        got[size - step] = behind
        got[step] = ahead
    got[half] = jnp.concatenate([behind, ahead], axis=1)
    return [got[k] for k in range(size)], done


def scatter_around(terms, axis, fillers):
    size = lax.axis_size(axis)
    half = size // 2
    width = terms[0].shape[1] // 2

    def step(first, second, filler):
        first = shift(first, axis, 1)
        second = shift(second, axis, -1)
        return lax.optimization_barrier((first, second, filler()))

    up, down, got = step(terms[half][:, :width], terms[half][:, width:], fillers[0])
    done = [got]
    up = jnp.concatenate([add_low(terms[half - 1][:, :width], up), terms[half - 1][:, width:]], 1)
    down = jnp.concatenate(
        [terms[half + 1][:, :width], add_low(terms[half + 1][:, width:], down)], 1
    )
    for ahead in range(half - 2, -1, -1):
        up, down, got = step(up, down, lambda: fillers[half - 1 - ahead](*done))
        done.append(got)
        if ahead:
            up = add_low(terms[ahead], up)
            down = add_low(terms[size - ahead], down)
    return up, down, done


def contract_rows(first_arg, second_arg):
    return lax.dot_general(
        first_arg, second_arg, (((0,), (0,)), ((), ())), preferred_element_type=F32
    )


def contract_cols(first_arg, second_arg):
    return lax.dot_general(
        first_arg, second_arg, (((1,), (1,)), ((), ())), preferred_element_type=F32
    )


def frame_row(row, lat_size):
    place = row + MARGIN
    return place // WLON * BAND + place % WLON * lat_size


def band_bias(lat_size):
    at = np.arange(BAND)
    group = np.where(at < WLON * lat_size, at % lat_size // WLAT, -1)
    return np.where(group[:, None] == group[None, :], 0.0, -1e30).astype(np.float32)


def merge_picks(lon_size, lat_size):
    picks = np.zeros((4, PAD, FRAME), np.float32)
    for i in range(lon_size // 2):
        for j in range(lat_size // 2):
            for a in range(2):
                for b in range(2):
                    picks[2 * a + b, i * (lat_size // 2) + j,
                          frame_row(2 * i + a, lat_size) + 2 * j + b] = 1.0
    return picks


def norm_parts(values):
    average = jnp.mean(values, axis=-1, keepdims=True)
    centred = values - average
    scale = lax.rsqrt(jnp.mean(centred * centred, axis=-1, keepdims=True) + EPSILON)
    return centred * scale, scale


def norm_back(unit, scale, grads):
    mean_grad = jnp.mean(grads, axis=-1, keepdims=True)
    mean_unit = jnp.mean(grads * unit, axis=-1, keepdims=True)
    return scale * (grads - mean_grad - unit * mean_unit)


def call(kernel, outs, scratch, flops, moved, *operands):
    specs = [
        pl.BlockSpec(memory_space=pltpu.SMEM) if operand.dtype == jnp.int32 else pl.BlockSpec()
        for operand in operands
    ]
    return pl.pallas_call(
        kernel,
        out_shape=outs,
        in_specs=specs,
        scratch_shapes=scratch,
        compiler_params=pltpu.CompilerParams(vmem_limit_bytes=60 * 1024 * 1024),
        cost_estimate=pl.CostEstimate(flops=flops, transcendentals=0, bytes_accessed=moved),
    )(*operands)


def head_masks():
    lane = lax.broadcasted_iota(jnp.int32, (1, 128), 1)
    return lane < 64, lane >= 64


def softmax_rows(scores):
    top = jnp.max(scores, axis=-1, keepdims=True)
    raised = jnp.exp(scores - top)
    return raised / jnp.sum(raised, axis=-1, keepdims=True)


def forward_kernel(west, field, east, bias, picks, qkv_w, out_w, gain_f, gain_m,
                   merged, rows, mixed, heads, frame, xs):
    lon_size, lat_size, channels = field.shape
    xs[...] = jnp.zeros_like(xs)
    for row in range(-MARGIN, lon_size + MARGIN):
        at = frame_row(row, lat_size)
        if row < 0:
            part = west[row + MARGIN]
        elif row < lon_size:
            part = field[row]
        else:
            part = east[row - lon_size]
        xs[at : at + lat_size, :] = part.astype(F32)
    values = xs[...]
    frame[...] = values.astype(BF)
    unit, _ = norm_parts(values)
    normed = (unit * gain_f[...]).astype(BF)
    mixed[...] = jnp.dot(normed, qkv_w[...], preferred_element_type=F32).astype(BF)
    masks = head_masks()
    scale = 1.0 / math.sqrt(channels // HEADS)
    for band in range(2):
        span = pl.ds(band * BAND, BAND)
        for pair in range(HEADS // 2):
            query = mixed[span, pair * 128 : (pair + 1) * 128]
            key = mixed[span, channels + pair * 128 : channels + (pair + 1) * 128]
            value = mixed[span, 2 * channels + pair * 128 : 2 * channels + (pair + 1) * 128]
            got = []
            for mask in masks:
                scores = contract_cols(jnp.where(mask, query, 0), key) * scale + bias[...]
                weights = softmax_rows(scores).astype(BF)
                got.append(jnp.dot(weights, value, preferred_element_type=F32))
            heads[span, pair * 128 : (pair + 1) * 128] = jnp.where(
                masks[0], got[0], got[1]
            ).astype(BF)
    attended = jnp.dot(heads[...], out_w[...], preferred_element_type=F32)
    field_out = (values + attended).astype(BF)
    for part in range(4):
        rows[:, part * channels : (part + 1) * channels] = jnp.dot(
            picks[part], field_out, preferred_element_type=F32
        ).astype(BF)
    unit, _ = norm_parts(rows[...].astype(F32))
    merged[...] = (unit * gain_m[...]).astype(BF)


def merge_back_kernel(rows, cot, back, back_up, back_down, gain_m, picks, d_frame, to_east, to_west, grad_gain):
    channels = d_frame.shape[1]
    unit, scale = norm_parts(rows[...].astype(F32))
    d_merged = cot[...].astype(F32) + (
        back[...].astype(F32) + back_up[...].astype(F32) + back_down[...].astype(F32)
    )
    grad_gain[...] = jnp.sum(d_merged * unit, axis=0, keepdims=True)
    d_rows = norm_back(unit, scale, d_merged * gain_m[...])
    high = d_rows.astype(BF)
    low = (d_rows - high.astype(F32)).astype(BF)
    total = jnp.zeros(d_frame.shape, F32)
    for part in range(4):
        cols = slice(part * channels, (part + 1) * channels)
        total += contract_rows(picks[part], high[:, cols])
        total += contract_rows(picks[part], low[:, cols])
    d_frame[...] = total
    span = to_east.shape[0]
    to_west[...] = d_frame[span : 2 * span, :].astype(BF)
    to_east[...] = d_frame[BAND : BAND + span, :].astype(BF)


def backward_kernel(core, frame, mixed, heads, d_frame, d_west, d_east, bias, qkv_w, out_w, gain_f,
                    gain_grad_m, grad_field, keep, give, dfl, d_mixed):
    lon_size, lat_size, channels = grad_field.shape
    span_rows = d_west.shape[0]
    dfl[...] = d_frame[...]
    dfl[0:span_rows, :] = d_west[...].astype(F32)
    dfl[BAND + span_rows : BAND + 2 * span_rows, :] = d_east[...].astype(F32)
    d_flat = dfl[...].astype(BF)
    d_heads = contract_cols(d_flat, out_w[...]).astype(BF)
    grad_out = contract_rows(heads[:BAND, :], d_flat[:BAND, :]).astype(BF)
    masks = head_masks()
    factor = 1.0 / math.sqrt(channels // HEADS)
    for band in range(2):
        span = pl.ds(band * BAND, BAND)
        for pair in range(HEADS // 2):
            cols = [slice(k * channels + pair * 128, k * channels + (pair + 1) * 128)
                    for k in range(3)]
            query, key, value = (mixed[span, c] for c in cols)
            d_out = d_heads[band * BAND : (band + 1) * BAND, cols[0]]
            got = []
            for mask in masks:
                own_query = jnp.where(mask, query, 0)
                scores = contract_cols(own_query, key) * factor + bias[...]
                weights = softmax_rows(scores)
                d_own = jnp.where(mask, d_out, 0)
                d_weights = contract_cols(d_own, value).astype(BF).astype(F32)
                d_value = contract_rows(weights.astype(BF), d_own)
                inner = jnp.sum(d_weights * weights, axis=-1, keepdims=True)
                d_scores = (weights * (d_weights - inner) * factor).astype(BF)
                d_query = jnp.dot(d_scores, key, preferred_element_type=F32)
                d_key = contract_rows(d_scores, own_query)
                got.append((d_query, d_key, d_value))
            for c, first, second in zip(cols, *got):
                d_mixed[span, c] = jnp.where(masks[0], first, second).astype(BF)
    unit, scale = norm_parts(frame[...].astype(F32))
    normed = (unit * gain_f[...]).astype(BF)
    grad_qkv = contract_rows(normed[:BAND, :], d_mixed[:BAND, :]).astype(BF)
    d_normed = contract_cols(d_mixed[...], qkv_w[...])
    grad_gain = jnp.sum(d_normed[:BAND, :] * unit[:BAND, :], axis=0, keepdims=True)
    dfl[...] = d_frame[...] + norm_back(unit, scale, d_normed * gain_f[...])
    for row in range(lon_size):
        at = frame_row(row, lat_size)
        grad_field[row] = dfl[at : at + lat_size, :]
    half = channels // 2
    top = lax.broadcasted_iota(jnp.int32, (16, 128), 0) == 0
    first = core[0] == 0
    for k in range(16):
        source, at = (grad_qkv, k) if k < 12 else (grad_out, k - 12)
        low = source[:half, at * 128 : (at + 1) * 128]
        high = source[half:, at * 128 : (at + 1) * 128]
        keep[k, 0:half, :] = jnp.where(first, low, high)
        give[k, 0:half, :] = jnp.where(first, high, low)
        low = jnp.where(top, gain_grad_m[:, k * 128 : (k + 1) * 128], 0.0)
        high = jnp.where(top, grad_gain[:, k * 128 : (k + 1) * 128], 0.0) if k < 4 else 0.0 * low
        keep[k, half : half + 16, :] = jnp.where(first, low, high).astype(BF)
        give[k, half : half + 16, :] = jnp.where(first, high, low).astype(BF)


def add_up_kernel(terms, total):
    acc = terms[0].astype(F32)
    for k in range(1, terms.shape[0]):
        acc += terms[k].astype(F32)
    total[...] = acc.astype(total.dtype)


def spread_kernel(core, mine, other, grad_qkv, grad_out, gain_f, gain_m):
    half = grad_out.shape[0] // 2
    for whose, part in ((core[0], mine), (1 - core[0], other)):
        own = pl.ds(pl.multiple_of(whose * half, half), half)
        for k in range(16):
            block = part[k, 0:half, :].astype(F32)
            if k < 12:
                grad_qkv[own, k * 128 : (k + 1) * 128] = block
            else:
                grad_out[own, (k - 12) * 128 : (k - 11) * 128] = block
    for k in range(16):
        pair = mine[k, half : half + 16, :].astype(F32), other[k, half : half + 16, :].astype(F32)
        first = jnp.where(core[0] == 0, pair[0], pair[1])
        gain_m[:, k * 128 : (k + 1) * 128] = first[0:1, :]
        if k < 4:
            second = jnp.where(core[0] == 0, pair[1], pair[0])
            gain_f[:, k * 128 : (k + 1) * 128] = second[0:1, :]


def stack_chunks(chunks, whole):
    gap = jnp.zeros((SLOT - PAD, whole.shape[1]), F32)
    for k, chunk in enumerate(chunks):
        filled = jnp.concatenate([chunk[...].astype(F32), gap], axis=0)
        whole[k * SLOT : (k + 1) * SLOT, :] = filled.astype(BF)


def join_halves(core, mine, other, whole):
    half = mine.shape[0]
    whole[pl.ds(pl.multiple_of(core * half, half), half), :] = mine[...]
    whole[pl.ds(pl.multiple_of((1 - core) * half, half), half), :] = other[...]


def gelu_parts(pre):
    slope = math.sqrt(2.0 / math.pi)
    square = pre * pre
    bent = jnp.tanh(slope * (pre + 0.044715 * square * pre))
    value = 0.5 * pre * (1.0 + bent)
    rate = slope * (1.0 + 3 * 0.044715 * square)
    return value, 0.5 * (1.0 + bent) + 0.5 * pre * (1.0 - bent * bent) * rate


def act_grad_kernel(place, core, chunks, own, mine, other, cot_all, d_act, shared):
    stack_chunks([chunks.at[lax.rem(place[0] + k, 8)] for k in range(8)], cot_all)
    join_halves(core[0], mine, other, shared)
    hidden = own.shape[0]
    for k, weight in enumerate((own, shared)):
        d_act[:, k * hidden : (k + 1) * hidden] = contract_cols(cot_all[...], weight[...])


def mlp_kernel(core, *refs):
    chunks, refs = refs[:8], refs[8:]
    (d_act, own, mine, other), refs = refs[:4], refs[4:]
    (merged_all, act, d_pre), refs = refs[:3], refs[3:]
    backs, (shared,) = refs[:8], refs[8:]
    stack_chunks(chunks, merged_all)
    join_halves(core[0], mine, other, shared)
    hidden = own.shape[1]
    for k, weight in enumerate((own, shared)):
        for at in range(0, hidden, 256):
            cols = slice(k * hidden + at, k * hidden + at + 256)
            pre = jnp.dot(merged_all[...], weight[:, at : at + 256], preferred_element_type=F32)
            value, slope = gelu_parts(pre)
            act[:, cols] = value.astype(BF)
            d_pre[:, cols] = (d_act[:, cols] * slope).astype(BF)
    for at in range(0, own.shape[0], 256):
        cols = slice(at, at + 256)
        term = contract_cols(d_pre[:, :hidden], own[cols, :])
        term += contract_cols(d_pre[:, hidden:], shared[cols, :])
        for k in range(8):
            backs[k][:, cols] = term[k * SLOT : k * SLOT + PAD, :].astype(BF)


def block_kernel(place, core, act, own, mine, other, terms, shared):
    join_halves(core[0], mine, other, shared)
    hidden = own.shape[0]
    for at in range(0, own.shape[1], 256):
        cols = slice(at, at + 256)
        term = jnp.dot(act[:, :hidden], own[:, cols], preferred_element_type=F32)
        term += jnp.dot(act[:, hidden:], shared[:, cols], preferred_element_type=F32)
        for k in range(8):
            terms[lax.rem(place[0] + k, 8), :, cols] = (
                term[k * SLOT : k * SLOT + PAD, :].astype(BF)
            )


def weight_grad_kernel(core, tokens, hidden, keep, give):
    for k in range(keep.shape[0]):
        both = contract_rows(tokens[:, k * 256 : (k + 1) * 256], hidden[...]).astype(BF)
        low, high = both[:128, :], both[128:, :]
        keep[k] = jnp.where(core[0] == 0, low, high)
        give[k] = jnp.where(core[0] == 0, high, low)


def shape(*size, of=BF):
    return jax.ShapeDtypeStruct(size, of)


def on_device(
    fine_field, qkv_weight, out_weight, gain_fine, gain_merge, up_weight, down_weight, cotangent
):
    core = lax.axis_index("c")
    whose = core.reshape(1)
    place = lax.axis_index("z").reshape(1)
    lon_size, lat_size, channels = fine_field.shape
    west = shift(fine_field[lon_size - MARGIN :], LON, 1)
    east = shift(fine_field[:MARGIN], LON, -1)

    grad_rows = cotangent.reshape(-1, 4 * channels)
    tokens = grad_rows.shape[0]
    grad_rows = jnp.pad(grad_rows, ((0, PAD - tokens), (0, 0)))
    grad_chunks = lax.all_gather(grad_rows, "z", axis=0)
    hidden = up_weight.shape[1]
    slots = 8 * SLOT

    halves = [part.shape[0] // 2 for part in (down_weight, up_weight)]
    west, east, down_mine, up_mine = lax.optimization_barrier((
        west,
        east,
        lax.dynamic_slice_in_dim(down_weight, core * halves[0], halves[0], 0),
        lax.dynamic_slice_in_dim(up_weight, core * halves[1], halves[1], 0),
    ))
    down_mine = swap(down_mine, "xl")
    up_mine = swap(up_mine, "xl")

    def act_grads(down_pair):
        return call(
            act_grad_kernel,
            (shape(slots, 4 * channels), shape(slots, 2 * hidden, of=F32)),
            [pltpu.VMEM((hidden, 4 * channels), BF)],
            2 * 10**9, 10**7,
            place, whose, grad_chunks, down_weight, *down_pair,
        )

    bias = jnp.asarray(band_bias(lat_size))
    picks = jnp.asarray(merge_picks(lon_size, lat_size), BF)
    gain_f = gain_fine.reshape(1, -1)
    gain_m = gain_merge.reshape(1, -1)
    merged, rows, mixed, heads, frame = call(
        forward_kernel,
        (shape(PAD, 4 * channels), shape(PAD, 4 * channels), shape(FRAME, 3 * channels),
         shape(FRAME, channels), shape(FRAME, channels)),
        [pltpu.VMEM((FRAME, channels), F32)],
        10**10, 8 * 10**6,
        west, fine_field, east, bias, picks, qkv_weight, out_weight, gain_f, gain_m,
    )
    merged_chunks, done = gather_around(
        merged,
        "z",
        [
            lambda: (),
            lambda first: down_mine,
            lambda first, second: (second, swap(second, "c"), up_mine),
            lambda first, second, third: (act_grads(third[:2]), swap(third[2], "c")),
        ],
    )
    down_mine, down_other, up_mine = done[2]
    (cot_all, d_act), up_other = done[3]
    merged_all, act, d_pre, *backs = call(
        mlp_kernel,
        (shape(slots, 4 * channels), shape(slots, 2 * hidden), shape(slots, 2 * hidden),
         *[shape(PAD, 4 * channels)] * 8),
        [pltpu.VMEM((4 * channels, hidden), BF)],
        5 * 10**9, 10**7,
        whose, *merged_chunks, d_act, up_weight, up_mine, up_other,
    )

    def weight_grad(rows, columns):
        keep, give = call(
            weight_grad_kernel,
            (shape(8, 128, 2 * hidden), shape(8, 128, 2 * hidden)),
            [],
            2 * 10**9, 10**7,
            whose, rows, columns,
        )
        return keep, give

    def far_half(pair):
        return add_low(pair[0][:, :, hidden:], pair[1][:, :, hidden:])

    def near_half(pair, far):
        near = pair[0][:, :, :hidden].astype(F32) + pair[1][:, :, :hidden].astype(F32)
        return (near + far.astype(F32)).astype(BF)

    def over_plane(pair):
        return lax.all_to_all(pair, ("y", "xh"), split_axis=0, concat_axis=0, tiled=True)

    def add_plane(terms):
        return call(add_up_kernel, shape(*terms.shape[1:], of=F32), [], 10**6, 10**6, terms)

    def block_terms():
        return call(
            block_kernel,
            shape(8, PAD, 4 * channels),
            [pltpu.VMEM((hidden, 4 * channels), BF)],
            2 * 10**9, 10**7,
            place, whose, act, down_weight, down_mine, down_other,
        )

    sent = {}

    def start_grad(name, rows, columns):
        keep, give = weight_grad(rows, columns)
        sent[name] = keep, swap(give, "c")
        return keep, give

    def start_far(name):
        far = far_half(sent[name])
        sent[name + "_far"] = swap(far, "xl")
        return far

    back_up, back_down, done = scatter_around(
        backs,
        "z",
        [
            lambda: start_grad("up", merged_all, d_pre),
            lambda first: (start_grad("down", cot_all, act), start_far("up")),
            lambda first, second: (far_half(sent["down"]), block_terms()),
            lambda first, second, third: (),
        ],
    )
    up_pair, down_pair = sent["up"], sent["down"]
    up_far = sent["up_far"]
    down_far, terms = done[2]
    summed = lax.psum_scatter(
        terms.reshape(8 * PAD, 4 * channels), "z", scatter_dimension=0, tiled=True
    )

    edge = MARGIN * lat_size
    d_frame, to_east, to_west, gain_grad_m = call(
        merge_back_kernel,
        (shape(FRAME, channels, of=F32), shape(edge, channels), shape(edge, channels),
         shape(1, 4 * channels, of=F32)),
        [],
        10**9, 2 * 10**6,
        rows, grad_rows, backs[0], back_up, back_down, gain_m, picks,
    )
    d_west = shift(to_east, LON, 1)
    d_east = shift(to_west, LON, -1)
    d_west, d_east, down_far, up_near = lax.optimization_barrier(
        (d_west, d_east, down_far, near_half(up_pair, up_far))
    )
    down_far = swap(down_far, "xl")
    up_terms = over_plane(up_near)
    size = (16, channels // 2 + 16, 128)
    grad_field, keep, give = call(
        backward_kernel,
        (shape(lon_size, lat_size, channels, of=F32), shape(*size), shape(*size)),
        [pltpu.VMEM((FRAME, channels), F32), pltpu.VMEM((FRAME, 3 * channels), BF)],
        2 * 10**10, 10**7,
        whose, frame, mixed, heads, d_frame, d_west, d_east, bias, qkv_weight, out_weight, gain_f,
        gain_grad_m,
    )
    keep, give, up_terms = lax.optimization_barrier((keep, give, up_terms))
    total = add_low(keep, swap(give, "c"))
    total = lax.all_to_all(total, PLANE, split_axis=0, concat_axis=0, tiled=True)
    total, down_far, summed = lax.optimization_barrier((total, down_far, summed))
    down_terms = over_plane(near_half(down_pair, down_far))
    bottleneck = (
        (merged[:tokens].astype(F32) + summed[:tokens].astype(F32))
        .astype(BF)
        .reshape(cotangent.shape)
    )
    total = call(add_up_kernel, shape(*size[1:]), [], 2 * 10**6, 2 * 10**6, total)
    for bit in (1, 2, 4):
        total = add_low(total, swap(total, "z", bit))
    total, down_terms = lax.optimization_barrier((total, down_terms))
    total = jnp.broadcast_to(total, size)
    mine = lax.all_to_all(total, PLANE, split_axis=0, concat_axis=0, tiled=True)
    other = swap(mine, "c")
    grad_up_part = add_plane(up_terms)
    grad_down_part = add_plane(down_terms).T
    grad_qkv, grad_out, grad_gain_fine, grad_gain_merge = call(
        spread_kernel,
        (shape(channels, 3 * channels, of=F32), shape(channels, channels, of=F32),
         shape(1, channels, of=F32), shape(1, 4 * channels, of=F32)),
        [],
        10**6, 5 * 10**6,
        whose, mine, other,
    )
    return (
        bottleneck,
        grad_field,
        grad_qkv,
        grad_out,
        grad_gain_fine.reshape(-1),
        grad_gain_merge.reshape(-1),
        grad_up_part,
        grad_down_part,
    )


def solution(mesh):
    torus = Mesh(mesh.devices.reshape(4, 2, 2, 8, 2), LON + LAT)
    placed = (
        P(LON, LAT, None),
        P(),
        P(),
        P(),
        P(),
        P(None, LAT),
        P(LAT, None),
        P(LON, LAT, None),
    )
    return jax.shard_map(
        on_device,
        mesh=torus,
        in_specs=placed,
        out_specs=(
            P(LON, LAT, None),
            P(LON, LAT, None),
            P(),
            P(),
            P(),
            P(),
            P(LON, LAT),
            P(LAT, LON),
        ),
        check_vma=False,
    )
```

```python
import math

import jax
import jax.numpy as jnp
import numpy as np
from jax import lax
from jax.experimental import pallas as pl
from jax.experimental.pallas import tpu as pltpu
from jax.sharding import Mesh
from jax.sharding import PartitionSpec as P

HEADS = 8
WLON = 12
WLAT = 6
MARGIN = WLON // 2
EPSILON = 1e-05
LON = ("y", "xh", "c")
LAT = ("z", "xl")
PLANE = ("y", "xh", "xl")
BF = jnp.bfloat16
F32 = jnp.float32
PAD = 56
SLOT = 64
BAND = 224
FRAME = 2 * BAND


def shift(block, axis, distance):
    size = lax.axis_size(axis)
    return lax.ppermute(block, axis, [(i, (i + distance) % size) for i in range(size)])


def swap(block, axis, bit=1):
    size = lax.axis_size(axis)
    return lax.ppermute(block, axis, [(i, i ^ bit) for i in range(size)])


def add_low(first_arg, second_arg):
    return (first_arg.astype(F32) + second_arg.astype(F32)).astype(BF)


def gather_around(block, axis, fillers):
    size = lax.axis_size(axis)
    half = size // 2
    width = block.shape[1] // 2
    got = {0: block}
    behind = ahead = block
    done = []
    for step in range(1, half + 1):
        if step == half:
            behind, ahead = behind[:, :width], ahead[:, width:]
        behind = shift(behind, axis, 1)
        ahead = shift(ahead, axis, -1)
        behind, ahead, extra = lax.optimization_barrier(
            (behind, ahead, fillers[step - 1](*done))
        )
        done.append(extra)
        got[size - step] = behind
        got[step] = ahead
    got[half] = jnp.concatenate([behind, ahead], axis=1)
    return [got[k] for k in range(size)], done


def scatter_around(terms, axis, fillers):
    size = lax.axis_size(axis)
    half = size // 2
    width = terms[0].shape[1] // 2

    def step(first, second, filler):
        first = shift(first, axis, 1)
        second = shift(second, axis, -1)
        return lax.optimization_barrier((first, second, filler()))

    up, down, got = step(terms[half][:, :width], terms[half][:, width:], fillers[0])
    done = [got]
    up = jnp.concatenate([add_low(terms[half - 1][:, :width], up), terms[half - 1][:, width:]], 1)
    down = jnp.concatenate(
        [terms[half + 1][:, :width], add_low(terms[half + 1][:, width:], down)], 1
    )
    for ahead in range(half - 2, -1, -1):
        up, down, got = step(up, down, lambda: fillers[half - 1 - ahead](*done))
        done.append(got)
        if ahead:
            up = add_low(terms[ahead], up)
            down = add_low(terms[size - ahead], down)
    return up, down, done


def contract_rows(first_arg, second_arg):
    return lax.dot_general(
        first_arg, second_arg, (((0,), (0,)), ((), ())), preferred_element_type=F32
    )


def contract_cols(first_arg, second_arg):
    return lax.dot_general(
        first_arg, second_arg, (((1,), (1,)), ((), ())), preferred_element_type=F32
    )


def frame_row(row, lat_size):
    place = row + MARGIN
    return place // WLON * BAND + place % WLON * lat_size


def band_bias(lat_size):
    at = np.arange(BAND)
    group = np.where(at < WLON * lat_size, at % lat_size // WLAT, -1)
    return np.where(group[:, None] == group[None, :], 0.0, -1e30).astype(np.float32)


def merge_picks(lon_size, lat_size):
    picks = np.zeros((4, PAD, FRAME), np.float32)
    for i in range(lon_size // 2):
        for j in range(lat_size // 2):
            for a in range(2):
                for b in range(2):
                    picks[2 * a + b, i * (lat_size // 2) + j,
                          frame_row(2 * i + a, lat_size) + 2 * j + b] = 1.0
    return picks


def norm_parts(values):
    average = jnp.mean(values, axis=-1, keepdims=True)
    centred = values - average
    scale = lax.rsqrt(jnp.mean(centred * centred, axis=-1, keepdims=True) + EPSILON)
    return centred * scale, scale


def norm_back(unit, scale, grads):
    mean_grad = jnp.mean(grads, axis=-1, keepdims=True)
    mean_unit = jnp.mean(grads * unit, axis=-1, keepdims=True)
    return scale * (grads - mean_grad - unit * mean_unit)


def call(kernel, outs, scratch, flops, moved, *operands):
    specs = [
        pl.BlockSpec(memory_space=pltpu.SMEM) if operand.dtype == jnp.int32 else pl.BlockSpec()
        for operand in operands
    ]
    return pl.pallas_call(
        kernel,
        out_shape=outs,
        in_specs=specs,
        scratch_shapes=scratch,
        compiler_params=pltpu.CompilerParams(vmem_limit_bytes=20 * 1024 * 1024),
        cost_estimate=pl.CostEstimate(flops=flops, transcendentals=0, bytes_accessed=moved),
    )(*operands)


def head_masks():
    lane = lax.broadcasted_iota(jnp.int32, (1, 128), 1)
    return lane < 64, lane >= 64


def softmax_rows(scores):
    top = jnp.max(scores, axis=-1, keepdims=True)
    raised = jnp.exp(scores - top)
    return raised / jnp.sum(raised, axis=-1, keepdims=True)


def forward_kernel(west, field, east, bias, picks, qkv_w, out_w, gain_f, gain_m,
                   merged, rows, mixed, heads, frame, xs):
    lon_size, lat_size, channels = field.shape
    xs[...] = jnp.zeros_like(xs)
    for row in range(-MARGIN, lon_size + MARGIN):
        at = frame_row(row, lat_size)
        if row < 0:
            part = west[row + MARGIN]
        elif row < lon_size:
            part = field[row]
        else:
            part = east[row - lon_size]
        xs[at : at + lat_size, :] = part.astype(F32)
    values = xs[...]
    frame[...] = values.astype(BF)
    unit, _ = norm_parts(values)
    normed = (unit * gain_f[...]).astype(BF)
    mixed[...] = jnp.dot(normed, qkv_w[...], preferred_element_type=F32).astype(BF)
    masks = head_masks()
    scale = 1.0 / math.sqrt(channels // HEADS)
    for band in range(2):
        span = pl.ds(band * BAND, BAND)
        for pair in range(HEADS // 2):
            query = mixed[span, pair * 128 : (pair + 1) * 128]
            key = mixed[span, channels + pair * 128 : channels + (pair + 1) * 128]
            value = mixed[span, 2 * channels + pair * 128 : 2 * channels + (pair + 1) * 128]
            got = []
            for mask in masks:
                scores = contract_cols(jnp.where(mask, query, 0), key) * scale + bias[...]
                weights = softmax_rows(scores).astype(BF)
                got.append(jnp.dot(weights, value, preferred_element_type=F32))
            heads[span, pair * 128 : (pair + 1) * 128] = jnp.where(
                masks[0], got[0], got[1]
            ).astype(BF)
    attended = jnp.dot(heads[...], out_w[...], preferred_element_type=F32)
    field_out = (values + attended).astype(BF)
    for part in range(4):
        rows[:, part * channels : (part + 1) * channels] = jnp.dot(
            picks[part], field_out, preferred_element_type=F32
        ).astype(BF)
    unit, _ = norm_parts(rows[...].astype(F32))
    merged[...] = (unit * gain_m[...]).astype(BF)


def merge_back_kernel(rows, cot, back, back_up, back_down, gain_m, picks, d_frame, to_east, to_west, grad_gain):
    channels = d_frame.shape[1]
    unit, scale = norm_parts(rows[...].astype(F32))
    d_merged = cot[...].astype(F32) + (
        back[...].astype(F32) + back_up[...].astype(F32) + back_down[...].astype(F32)
    )
    grad_gain[...] = jnp.sum(d_merged * unit, axis=0, keepdims=True)
    d_rows = norm_back(unit, scale, d_merged * gain_m[...])
    high = d_rows.astype(BF)
    low = (d_rows - high.astype(F32)).astype(BF)
    total = jnp.zeros(d_frame.shape, F32)
    for part in range(4):
        cols = slice(part * channels, (part + 1) * channels)
        total += contract_rows(picks[part], high[:, cols])
        total += contract_rows(picks[part], low[:, cols])
    d_frame[...] = total
    span = to_east.shape[0]
    to_west[...] = d_frame[span : 2 * span, :].astype(BF)
    to_east[...] = d_frame[BAND : BAND + span, :].astype(BF)


def backward_kernel(core, frame, mixed, heads, d_frame, d_west, d_east, bias, qkv_w, out_w, gain_f,
                    gain_grad_m, grad_field, keep, give, dfl, d_mixed):
    lon_size, lat_size, channels = grad_field.shape
    span_rows = d_west.shape[0]
    dfl[...] = d_frame[...]
    dfl[0:span_rows, :] = d_west[...].astype(F32)
    dfl[BAND + span_rows : BAND + 2 * span_rows, :] = d_east[...].astype(F32)
    d_flat = dfl[...].astype(BF)
    d_heads = contract_cols(d_flat, out_w[...]).astype(BF)
    grad_out = contract_rows(heads[:BAND, :], d_flat[:BAND, :]).astype(BF)
    masks = head_masks()
    factor = 1.0 / math.sqrt(channels // HEADS)
    for band in range(2):
        span = pl.ds(band * BAND, BAND)
        for pair in range(HEADS // 2):
            cols = [slice(k * channels + pair * 128, k * channels + (pair + 1) * 128)
                    for k in range(3)]
            query, key, value = (mixed[span, c] for c in cols)
            d_out = d_heads[band * BAND : (band + 1) * BAND, cols[0]]
            got = []
            for mask in masks:
                own_query = jnp.where(mask, query, 0)
                scores = contract_cols(own_query, key) * factor + bias[...]
                weights = softmax_rows(scores)
                d_own = jnp.where(mask, d_out, 0)
                d_weights = contract_cols(d_own, value).astype(BF).astype(F32)
                d_value = contract_rows(weights.astype(BF), d_own)
                inner = jnp.sum(d_weights * weights, axis=-1, keepdims=True)
                d_scores = (weights * (d_weights - inner) * factor).astype(BF)
                d_query = jnp.dot(d_scores, key, preferred_element_type=F32)
                d_key = contract_rows(d_scores, own_query)
                got.append((d_query, d_key, d_value))
            for c, first, second in zip(cols, *got):
                d_mixed[span, c] = jnp.where(masks[0], first, second).astype(BF)
    unit, scale = norm_parts(frame[...].astype(F32))
    normed = (unit * gain_f[...]).astype(BF)
    grad_qkv = contract_rows(normed[:BAND, :], d_mixed[:BAND, :]).astype(BF)
    d_normed = contract_cols(d_mixed[...], qkv_w[...])
    grad_gain = jnp.sum(d_normed[:BAND, :] * unit[:BAND, :], axis=0, keepdims=True)
    dfl[...] = d_frame[...] + norm_back(unit, scale, d_normed * gain_f[...])
    for row in range(lon_size):
        at = frame_row(row, lat_size)
        grad_field[row] = dfl[at : at + lat_size, :]
    half = channels // 2
    top = lax.broadcasted_iota(jnp.int32, (16, 128), 0) == 0
    first = core[0] == 0
    for k in range(16):
        source, at = (grad_qkv, k) if k < 12 else (grad_out, k - 12)
        low = source[:half, at * 128 : (at + 1) * 128]
        high = source[half:, at * 128 : (at + 1) * 128]
        keep[k, 0:half, :] = jnp.where(first, low, high)
        give[k, 0:half, :] = jnp.where(first, high, low)
        low = jnp.where(top, gain_grad_m[:, k * 128 : (k + 1) * 128], 0.0)
        high = jnp.where(top, grad_gain[:, k * 128 : (k + 1) * 128], 0.0) if k < 4 else 0.0 * low
        keep[k, half : half + 16, :] = jnp.where(first, low, high).astype(BF)
        give[k, half : half + 16, :] = jnp.where(first, high, low).astype(BF)


def add_up_kernel(terms, total):
    acc = terms[0].astype(F32)
    for k in range(1, terms.shape[0]):
        acc += terms[k].astype(F32)
    total[...] = acc.astype(total.dtype)


def spread_kernel(core, mine, other, grad_qkv, grad_out, gain_f, gain_m):
    half = grad_out.shape[0] // 2
    for whose, part in ((core[0], mine), (1 - core[0], other)):
        own = pl.ds(pl.multiple_of(whose * half, half), half)
        for k in range(16):
            block = part[k, 0:half, :].astype(F32)
            if k < 12:
                grad_qkv[own, k * 128 : (k + 1) * 128] = block
            else:
                grad_out[own, (k - 12) * 128 : (k - 11) * 128] = block
    for k in range(16):
        pair = mine[k, half : half + 16, :].astype(F32), other[k, half : half + 16, :].astype(F32)
        first = jnp.where(core[0] == 0, pair[0], pair[1])
        gain_m[:, k * 128 : (k + 1) * 128] = first[0:1, :]
        if k < 4:
            second = jnp.where(core[0] == 0, pair[1], pair[0])
            gain_f[:, k * 128 : (k + 1) * 128] = second[0:1, :]


def stack_chunks(chunks, whole):
    gap = jnp.zeros((SLOT - PAD, whole.shape[1]), F32)
    for k, chunk in enumerate(chunks):
        filled = jnp.concatenate([chunk[...].astype(F32), gap], axis=0)
        whole[k * SLOT : (k + 1) * SLOT, :] = filled.astype(BF)


def join_halves(core, mine, other, whole):
    half = mine.shape[0]
    whole[pl.ds(pl.multiple_of(core * half, half), half), :] = mine[...]
    whole[pl.ds(pl.multiple_of((1 - core) * half, half), half), :] = other[...]


def gelu_parts(pre):
    slope = math.sqrt(2.0 / math.pi)
    square = pre * pre
    bent = jnp.tanh(slope * (pre + 0.044715 * square * pre))
    value = 0.5 * pre * (1.0 + bent)
    rate = slope * (1.0 + 3 * 0.044715 * square)
    return value, 0.5 * (1.0 + bent) + 0.5 * pre * (1.0 - bent * bent) * rate


def act_grad_kernel(place, core, chunks, own, mine, other, cot_all, d_act, shared):
    stack_chunks([chunks.at[lax.rem(place[0] + k, 8)] for k in range(8)], cot_all)
    join_halves(core[0], mine, other, shared)
    hidden = own.shape[0]
    for k, weight in enumerate((own, shared)):
        d_act[:, k * hidden : (k + 1) * hidden] = contract_cols(cot_all[...], weight[...])


def mlp_kernel(core, *refs):
    chunks, refs = refs[:8], refs[8:]
    (d_act, own, mine, other), refs = refs[:4], refs[4:]
    (merged_all, act, d_pre), refs = refs[:3], refs[3:]
    backs, (shared,) = refs[:8], refs[8:]
    stack_chunks(chunks, merged_all)
    join_halves(core[0], mine, other, shared)
    hidden = own.shape[1]
    for k, weight in enumerate((own, shared)):
        for at in range(0, hidden, 256):
            cols = slice(k * hidden + at, k * hidden + at + 256)
            pre = jnp.dot(merged_all[...], weight[:, at : at + 256], preferred_element_type=F32)
            value, slope = gelu_parts(pre)
            act[:, cols] = value.astype(BF)
            d_pre[:, cols] = (d_act[:, cols] * slope).astype(BF)
    for at in range(0, own.shape[0], 256):
        cols = slice(at, at + 256)
        term = contract_cols(d_pre[:, :hidden], own[cols, :])
        term += contract_cols(d_pre[:, hidden:], shared[cols, :])
        for k in range(8):
            backs[k][:, cols] = term[k * SLOT : k * SLOT + PAD, :].astype(BF)


def block_kernel(place, core, act, own, mine, other, terms, shared):
    join_halves(core[0], mine, other, shared)
    hidden = own.shape[0]
    for at in range(0, own.shape[1], 256):
        cols = slice(at, at + 256)
        term = jnp.dot(act[:, :hidden], own[:, cols], preferred_element_type=F32)
        term += jnp.dot(act[:, hidden:], shared[:, cols], preferred_element_type=F32)
        for k in range(8):
            terms[lax.rem(place[0] + k, 8), :, cols] = (
                term[k * SLOT : k * SLOT + PAD, :].astype(BF)
            )


def weight_grad_kernel(core, tokens, hidden, keep, give):
    for k in range(keep.shape[0]):
        both = contract_rows(tokens[:, k * 256 : (k + 1) * 256], hidden[...]).astype(BF)
        low, high = both[:128, :], both[128:, :]
        keep[k] = jnp.where(core[0] == 0, low, high)
        give[k] = jnp.where(core[0] == 0, high, low)


def shape(*size, of=BF):
    return jax.ShapeDtypeStruct(size, of)


def on_device(
    fine_field, qkv_weight, out_weight, gain_fine, gain_merge, up_weight, down_weight, cotangent
):
    core = lax.axis_index("c")
    whose = core.reshape(1)
    place = lax.axis_index("z").reshape(1)
    lon_size, lat_size, channels = fine_field.shape
    west = shift(fine_field[lon_size - MARGIN :], LON, 1)
    east = shift(fine_field[:MARGIN], LON, -1)

    grad_rows = cotangent.reshape(-1, 4 * channels)
    tokens = grad_rows.shape[0]
    grad_rows = jnp.pad(grad_rows, ((0, PAD - tokens), (0, 0)))
    grad_chunks = lax.all_gather(grad_rows, "z", axis=0)
    hidden = up_weight.shape[1]
    slots = 8 * SLOT

    halves = [part.shape[0] // 2 for part in (down_weight, up_weight)]
    west, east, down_mine, up_mine = lax.optimization_barrier((
        west,
        east,
        lax.dynamic_slice_in_dim(down_weight, core * halves[0], halves[0], 0),
        lax.dynamic_slice_in_dim(up_weight, core * halves[1], halves[1], 0),
    ))
    down_mine = swap(down_mine, "xl")
    up_mine = swap(up_mine, "xl")

    def act_grads(down_pair):
        return call(
            act_grad_kernel,
            (shape(slots, 4 * channels), shape(slots, 2 * hidden, of=F32)),
            [pltpu.VMEM((hidden, 4 * channels), BF)],
            2 * 10**9, 10**7,
            place, whose, grad_chunks, down_weight, *down_pair,
        )

    bias = jnp.asarray(band_bias(lat_size))
    picks = jnp.asarray(merge_picks(lon_size, lat_size), BF)
    gain_f = gain_fine.reshape(1, -1)
    gain_m = gain_merge.reshape(1, -1)
    merged, rows, mixed, heads, frame = call(
        forward_kernel,
        (shape(PAD, 4 * channels), shape(PAD, 4 * channels), shape(FRAME, 3 * channels),
         shape(FRAME, channels), shape(FRAME, channels)),
        [pltpu.VMEM((FRAME, channels), F32)],
        10**10, 8 * 10**6,
        west, fine_field, east, bias, picks, qkv_weight, out_weight, gain_f, gain_m,
    )
    merged_chunks, done = gather_around(
        merged,
        "z",
        [
            lambda: (),
            lambda first: down_mine,
            lambda first, second: (second, swap(second, "c"), up_mine),
            lambda first, second, third: (act_grads(third[:2]), swap(third[2], "c")),
        ],
    )
    down_mine, down_other, up_mine = done[2]
    (cot_all, d_act), up_other = done[3]
    merged_all, act, d_pre, *backs = call(
        mlp_kernel,
        (shape(slots, 4 * channels), shape(slots, 2 * hidden), shape(slots, 2 * hidden),
         *[shape(PAD, 4 * channels)] * 8),
        [pltpu.VMEM((4 * channels, hidden), BF)],
        5 * 10**9, 10**7,
        whose, *merged_chunks, d_act, up_weight, up_mine, up_other,
    )

    def weight_grad(rows, columns):
        keep, give = call(
            weight_grad_kernel,
            (shape(8, 128, 2 * hidden), shape(8, 128, 2 * hidden)),
            [],
            2 * 10**9, 10**7,
            whose, rows, columns,
        )
        return keep, give

    def far_half(pair):
        return add_low(pair[0][:, :, hidden:], pair[1][:, :, hidden:])

    def near_half(pair, far):
        near = pair[0][:, :, :hidden].astype(F32) + pair[1][:, :, :hidden].astype(F32)
        return (near + far.astype(F32)).astype(BF)

    def over_plane(pair):
        return lax.all_to_all(pair, ("y", "xh"), split_axis=0, concat_axis=0, tiled=True)

    def add_plane(terms):
        return call(add_up_kernel, shape(*terms.shape[1:], of=F32), [], 10**6, 10**6, terms)

    def block_terms():
        return call(
            block_kernel,
            shape(8, PAD, 4 * channels),
            [pltpu.VMEM((hidden, 4 * channels), BF)],
            2 * 10**9, 10**7,
            place, whose, act, down_weight, down_mine, down_other,
        )

    sent = {}

    def start_grad(name, rows, columns):
        keep, give = weight_grad(rows, columns)
        sent[name] = keep, swap(give, "c")
        return keep, give

    def start_far(name):
        far = far_half(sent[name])
        sent[name + "_far"] = swap(far, "xl")
        return far

    back_up, back_down, done = scatter_around(
        backs,
        "z",
        [
            lambda: start_grad("up", merged_all, d_pre),
            lambda first: (start_grad("down", cot_all, act), start_far("up")),
            lambda first, second: (far_half(sent["down"]), block_terms()),
            lambda first, second, third: (),
        ],
    )
    up_pair, down_pair = sent["up"], sent["down"]
    up_far = sent["up_far"]
    down_far, terms = done[2]
    summed = lax.psum_scatter(
        terms.reshape(8 * PAD, 4 * channels), "z", scatter_dimension=0, tiled=True
    )

    edge = MARGIN * lat_size
    d_frame, to_east, to_west, gain_grad_m = call(
        merge_back_kernel,
        (shape(FRAME, channels, of=F32), shape(edge, channels), shape(edge, channels),
         shape(1, 4 * channels, of=F32)),
        [],
        10**9, 2 * 10**6,
        rows, grad_rows, backs[0], back_up, back_down, gain_m, picks,
    )
    d_west = shift(to_east, LON, 1)
    d_east = shift(to_west, LON, -1)
    d_west, d_east, down_far, up_near = lax.optimization_barrier(
        (d_west, d_east, down_far, near_half(up_pair, up_far))
    )
    down_far = swap(down_far, "xl")
    up_terms = over_plane(up_near)
    size = (16, channels // 2 + 16, 128)
    grad_field, keep, give = call(
        backward_kernel,
        (shape(lon_size, lat_size, channels, of=F32), shape(*size), shape(*size)),
        [pltpu.VMEM((FRAME, channels), F32), pltpu.VMEM((FRAME, 3 * channels), BF)],
        2 * 10**10, 10**7,
        whose, frame, mixed, heads, d_frame, d_west, d_east, bias, qkv_weight, out_weight, gain_f,
        gain_grad_m,
    )
    keep, give, up_terms = lax.optimization_barrier((keep, give, up_terms))
    total = add_low(keep, swap(give, "c"))
    total = lax.all_to_all(total, PLANE, split_axis=0, concat_axis=0, tiled=True)
    total, down_far, summed = lax.optimization_barrier((total, down_far, summed))
    down_terms = over_plane(near_half(down_pair, down_far))
    bottleneck = (
        (merged[:tokens].astype(F32) + summed[:tokens].astype(F32))
        .astype(BF)
        .reshape(cotangent.shape)
    )
    total = call(add_up_kernel, shape(*size[1:]), [], 2 * 10**6, 2 * 10**6, total)
    for bit in (1, 2, 4):
        total = add_low(total, swap(total, "z", bit))
    total, down_terms = lax.optimization_barrier((total, down_terms))
    total = jnp.broadcast_to(total, size)
    mine = lax.all_to_all(total, PLANE, split_axis=0, concat_axis=0, tiled=True)
    other = swap(mine, "c")
    grad_up_part = add_plane(up_terms)
    grad_down_part = add_plane(down_terms).T
    grad_qkv, grad_out, grad_gain_fine, grad_gain_merge = call(
        spread_kernel,
        (shape(channels, 3 * channels, of=F32), shape(channels, channels, of=F32),
         shape(1, channels, of=F32), shape(1, 4 * channels, of=F32)),
        [],
        10**6, 5 * 10**6,
        whose, mine, other,
    )
    return (
        bottleneck,
        grad_field,
        grad_qkv,
        grad_out,
        grad_gain_fine.reshape(-1),
        grad_gain_merge.reshape(-1),
        grad_up_part,
        grad_down_part,
    )


def solution(mesh):
    torus = Mesh(mesh.devices.reshape(4, 2, 2, 8, 2), LON + LAT)
    placed = (
        P(LON, LAT, None),
        P(),
        P(),
        P(),
        P(),
        P(None, LAT),
        P(LAT, None),
        P(LON, LAT, None),
    )
    return jax.shard_map(
        on_device,
        mesh=torus,
        in_specs=placed,
        out_specs=(
            P(LON, LAT, None),
            P(LON, LAT, None),
            P(),
            P(),
            P(),
            P(),
            P(LON, LAT),
            P(LAT, LON),
        ),
        check_vma=False,
    )
```
